32 devices in a mesh: rows: 8 (over z, y), cols: 4 (over x, core).
Axes of the slice: x: 2, y: 2, z: 4, core: 2. Of those that a mesh axis runs over, the one named last changes fastest.
Arguments:
- hblocks: float32 [64, 24, 128, 128], P('rows'), may hold values from -0.0546875 to 0.0546875
- col_index: int32 [64, 24], P('rows'), may hold values from 0 to 63, as said below
- right_side: float32 [64, 64, 128], P('rows', 'cols'), may hold values from -12 to 12
- center: float32 [1], replicated, may hold values from -0.5 to 0.5
- shifts: float32 [8], replicated, may hold values from 0.05 to 2
- filter_weights: float32 [8], replicated, may hold values from 0.03 to 0.3
Outputs:
- filtered: float32 [64, 64, 128], P('rows', 'cols')
- gram_matrix: float32 [64, 64], P(None, 'cols')
- ritz_matrix: float32 [64, 64], P(None, 'cols')
The draws below stay inside these ranges and needn't reach their ends.
Inputs may be any that keep to these rules, and one draw needn't show every extreme that they name: `col_index`: block rows are held 8 to a device of rows, in order. In block row i the first 8 column indices are the 8 block rows of the device that holds i, each once. Every other column index of a block row lies on another device of rows; for each pair of distinct devices, the block rows of the one that are named by the block rows of the other are exactly 2 distinct ones.
All inputs are finite; a program needn't handle non-finite values.
Results may differ from the reference program's by a relative error of at most 0.0001.
Values sent between devices are 32-bit elements; how exact they have to be, the bound alone decides.
A program may use at most 64 MiB of HBM per device.

```python
import math
import jax
import jax.numpy as jnp
from jax import lax

BLK = 128
NBLK = 24
NVEC = 64
POLES = 8
BR_DEV = 8
CAP = 2
ITERS = 2
NB = 64
N_ROWS = 8


def build_pattern(key):
    list_keys = jax.random.split(jax.random.fold_in(key, 7), N_ROWS * N_ROWS)
    shuffled = jax.vmap(lambda one_key: jax.random.permutation(one_key, BR_DEV))(list_keys)
    chosen = shuffled[:, :CAP].reshape(N_ROWS, N_ROWS, CAP).astype(jnp.int32)
    slot_total = (N_ROWS - 1) * CAP
    far_total = BR_DEV * (NBLK - BR_DEV)

    def one_device(device, device_key):
        extra_slots = jax.random.randint(jax.random.fold_in(device_key, 1), (far_total,), 0, slot_total, dtype=jnp.int32)
        counter = jnp.arange(far_total, dtype=jnp.int32)
        assigned = jnp.where(counter < slot_total, counter, extra_slots)
        assigned = jax.random.permutation(jax.random.fold_in(device_key, 2), assigned)
        owner_dev = assigned // CAP
        owner_dev = owner_dev + (owner_dev >= device).astype(jnp.int32)
        far_cols = owner_dev * BR_DEV + chosen[owner_dev, device, assigned % CAP]
        row_keys = jax.random.split(jax.random.fold_in(device_key, 3), BR_DEV)
        near_cols = jax.vmap(lambda one_key: jax.random.permutation(one_key, BR_DEV))(row_keys) + device * BR_DEV
        return jnp.concatenate([near_cols.astype(jnp.int32), far_cols.reshape(BR_DEV, NBLK - BR_DEV).astype(jnp.int32)], axis=1)
    device_keys = jax.random.split(jax.random.fold_in(key, 11), N_ROWS)
    columns = jax.vmap(one_device)(jnp.arange(N_ROWS, dtype=jnp.int32), device_keys)
    return columns.reshape(NB, NBLK)


def draw_col_index(key, part):
    return build_pattern(key)


def draw_right_side(key, part):
    position = jnp.arange(NB, dtype=jnp.float32)
    row_ramp = 1.0 + 2.0 * position / max(NB - 1, 1)
    row_rough = jnp.exp(jnp.log(2.0) * jax.random.uniform(jax.random.fold_in(key, 1), (NB, 1, 1)))
    col_rough = jnp.exp(jnp.log(2.0) * jax.random.uniform(jax.random.fold_in(key, 2), (1, NVEC, 1)))
    values = jax.random.normal(jax.random.fold_in(key, 3), (NB, NVEC, BLK))
    values = jnp.clip(values, -4.0, 4.0)
    return (values * row_ramp[:, None, None] * row_rough * col_rough / 4.0).astype(jnp.float32)


def block_levels(own_key, dims, cuts, smallest, top_value):
    def one(dim, blocks):
        heights = jax.random.uniform(jax.random.fold_in(jax.random.fold_in(own_key, 6), dim), (blocks,), jnp.float32, smallest / len(cuts), top_value / len(cuts))
        return jnp.repeat(jnp.exp(heights), dims[dim] // blocks).reshape((-1,) + (1,) * (len(dims) - dim - 1))

    loudness = one(*cuts[0])
    for cut in cuts[1:]:
        loudness = loudness * one(*cut)
    return loudness


def normal_values(rng, dims, spread, most, pieces=(), kind=jnp.bfloat16):
    values = jax.random.normal(rng, dims, jnp.float32) * spread
    if len(pieces) > 0:
        values = block_levels(rng, dims, pieces, -0.22, 0.18) * values
    return jnp.clip(values, min=-most, max=most).astype(kind)


def setup_inputs(seed: int = 0) -> dict:
    splits = jax.random.split(jax.random.key(seed), 7)
    return {
        "hblocks": normal_values(splits[0], (NB, NBLK, BLK, BLK), (4 * NBLK * BLK) ** -0.5, 0.0546875, ((0, 8),), jnp.float32),
        "col_index": draw_col_index(jax.random.fold_in(splits[6], 71), 0),
        "right_side": draw_right_side(jax.random.fold_in(splits[6], 71), 0),
        "center": jnp.clip(jax.random.uniform(splits[3], (1,), jnp.float32, -0.5, 0.5), -0.5, 0.5),
        "shifts": jnp.clip(jnp.exp(jax.random.uniform(splits[4], (POLES,), jnp.float32, math.log(0.05), math.log(2.0))), 0.05, 2.0),
        "filter_weights": jnp.clip(jnp.exp(jax.random.uniform(splits[5], (POLES,), jnp.float32, math.log(0.03), math.log(0.3))), 0.03, 0.3),
    }


exact_mode = lax.Precision.HIGHEST


def apply_h(vector, hblocks, col_index):
    gathered = vector[col_index]
    forward = jnp.einsum("ikab,ikvb->iva", hblocks, gathered, precision=exact_mode)
    transposed = jnp.einsum("ikab,iva->ikvb", hblocks, vector, precision=exact_mode)
    backward = jax.ops.segment_sum(transposed.reshape(-1, vector.shape[1], vector.shape[2]), col_index.reshape(-1), num_segments=vector.shape[0])
    return forward + backward


def column_dot(first_arr, second_arr):
    return jnp.sum(first_arr * second_arr, axis=(0, 2))


def reference(hblocks, col_index, right_side, center, shifts, filter_weights):
    center_value = center[0]
    base_shift = jnp.min(shifts)
    delta_shift = (shifts - base_shift)[:, None]

    def operate(vector):
        shifted = apply_h(vector, hblocks, col_index) - center_value * vector
        return apply_h(shifted, hblocks, col_index) - center_value * shifted + base_shift * vector

    residual = right_side
    direction = right_side
    solutions = jnp.zeros((POLES,) + right_side.shape, jnp.float32)
    shifted_dirs = jnp.broadcast_to(right_side, solutions.shape)
    res_norm = column_dot(residual, residual)
    zeta_prev = jnp.ones((POLES, NVEC), jnp.float32)
    zeta_now = jnp.ones((POLES, NVEC), jnp.float32)
    alpha_prev = jnp.ones((NVEC,), jnp.float32)
    beta_prev = jnp.zeros((NVEC,), jnp.float32)
    for iteration in range(ITERS):
        op_image = operate(direction)
        alpha_now = res_norm / column_dot(direction, op_image)
        zeta_next = zeta_now * zeta_prev * alpha_prev / (alpha_now * beta_prev * (zeta_prev - zeta_now) + zeta_prev * alpha_prev * (1.0 + delta_shift * alpha_now))
        zeta_ratio = zeta_next / zeta_now
        solutions = solutions + (alpha_now * zeta_ratio)[:, None, :, None] * shifted_dirs
        residual = residual - alpha_now[None, :, None] * op_image
        if iteration + 1 < ITERS:
            norm_next = column_dot(residual, residual)
            beta_now = norm_next / res_norm
            direction = residual + beta_now[None, :, None] * direction
            shifted_dirs = zeta_next[:, None, :, None] * residual[None] + (beta_now * zeta_ratio * zeta_ratio)[:, None, :, None] * shifted_dirs
            zeta_prev, zeta_now, alpha_prev, beta_prev, res_norm = zeta_now, zeta_next, alpha_now, beta_now, norm_next
    filtered = jnp.sum(filter_weights[:, None, None, None] * solutions, axis=0)
    applied = apply_h(filtered, hblocks, col_index)
    row_total = NB * BLK
    gram_matrix = jnp.einsum("iae,ibe->ab", filtered, filtered, precision=exact_mode) / row_total
    ritz_matrix = jnp.einsum("iae,ibe->ab", filtered, applied, precision=exact_mode) / row_total
    return filtered, gram_matrix, ritz_matrix
```

```python
import functools

import jax
import jax.numpy as jnp
from jax import lax
from jax.experimental import pallas as pl
from jax.experimental.pallas import tpu as pltpu
from jax.sharding import PartitionSpec as P

CAP = 2


exact_mode = lax.Precision.HIGHEST


def column_dot(first_arr, second_arr):
    return jnp.sum(first_arr * second_arr, axis=(0, 2))


def ordered_lists(need_mask, slot_width):
    ranks = jnp.cumsum(need_mask, axis=1)
    positions = lax.broadcasted_iota(jnp.int32, need_mask.shape, 1)
    columns_out = []
    for slot in range(slot_width):
        hit = (need_mask > 0) & (ranks == slot + 1)
        columns_out.append(jnp.sum(jnp.where(hit, positions, 0), axis=1))
    lists = jnp.stack(columns_out, axis=1)
    live = jnp.sum(need_mask, axis=1, keepdims=True) > 0
    return jnp.where(live, lists, -1)


def filter_factors(alpha_one, beta_one, alpha_two, delta_shift, weights):
    zeta_one = 1.0 / (1.0 + delta_shift * alpha_one)
    zeta_two = (
        zeta_one
        * alpha_one
        / (alpha_two * beta_one * (1.0 - zeta_one) + alpha_one * (1.0 + delta_shift * alpha_two))
    )
    from_start = jnp.sum(
        weights * (alpha_one * zeta_one + alpha_two * beta_one * zeta_one * zeta_two), axis=0
    )
    from_residual = jnp.sum(weights * (alpha_two * zeta_two), axis=0)
    return from_start, from_residual


def shards(hblocks, col_index, right_side, center, shifts, filter_weights):
    block_rows = hblocks.shape[0]
    block_width = hblocks.shape[2]
    local_vecs = right_side.shape[1]
    pole_count = shifts.shape[0]
    peer_count = lax.axis_size("rows")
    slot_width = CAP
    device_index = lax.axis_index("rows")
    own_cols = col_index[:, :block_rows] - device_index * block_rows
    far_cols = col_index[:, block_rows:].reshape(-1)
    near_blocks = hblocks[:, :block_rows]
    far_blocks = hblocks[:, block_rows:]
    every_key = jnp.arange(peer_count * block_rows, dtype=jnp.int32)
    need_mask = (
        jnp.any(far_cols[:, None] == every_key[None, :], axis=0)
        .astype(jnp.int32)
        .reshape(peer_count, block_rows)
    )
    incoming_mask = lax.all_to_all(need_mask, "rows", split_axis=0, concat_axis=0, tiled=True)
    send_lists = ordered_lists(incoming_mask, slot_width)
    my_lists = ordered_lists(need_mask, slot_width)
    owners = lax.broadcasted_iota(jnp.int32, my_lists.shape, 0)
    slot_keys = jnp.where(my_lists >= 0, owners * block_rows + my_lists, -1).reshape(-1)
    slot_total = slot_keys.shape[0]
    matches = far_cols[:, None] == slot_keys[None, :]
    picker = matches.astype(jnp.float32)
    slot_numbers = lax.broadcasted_iota(jnp.int32, matches.shape, 1)
    slot_of_ref = jnp.sum(jnp.where(matches, slot_numbers, 0), axis=1)
    row_numbers = jnp.arange(block_rows, dtype=jnp.int32)[:, None]
    spread = (send_lists.reshape(-1)[None, :] == row_numbers).astype(jnp.float32)
    own_spread = (own_cols.reshape(-1)[None, :] == row_numbers).astype(jnp.float32)
    send_index = jnp.maximum(send_lists, 0)
    send_live = (send_lists >= 0)[:, :, None, None]

    def apply_h(vector):
        far_terms = jnp.einsum("ikab,iva->ikvb", far_blocks, vector, precision=exact_mode).reshape(
            far_cols.shape[0], -1
        )
        slot_sums = jnp.dot(picker.T, far_terms, precision=exact_mode).reshape(
            peer_count, slot_width, local_vecs, block_width
        )
        picked = vector[send_index]
        outgoing = jnp.where(send_live, picked, jnp.zeros_like(picked))
        both = lax.all_to_all(
            jnp.concatenate([outgoing, slot_sums], axis=1),
            "rows",
            split_axis=0,
            concat_axis=0,
            tiled=True,
        )
        arrived = both[:, :slot_width].reshape(slot_total, local_vecs, block_width)
        returned = both[:, slot_width:].reshape(slot_total, -1)
        near_vec = vector[own_cols]
        result = jnp.einsum("ikab,ikvb->iva", near_blocks, near_vec, precision=exact_mode)
        near_terms = jnp.einsum(
            "ikab,iva->ikvb", near_blocks, vector, precision=exact_mode
        ).reshape(block_rows * block_rows, -1)
        result = result + jnp.dot(own_spread, near_terms, precision=exact_mode).reshape(
            vector.shape
        )
        far_vec = arrived[slot_of_ref]
        far_vec = far_vec.reshape(block_rows, -1, local_vecs, block_width)
        result = result + jnp.einsum("ikab,ikvb->iva", far_blocks, far_vec, precision=exact_mode)
        return result + jnp.dot(spread, returned, precision=exact_mode).reshape(vector.shape)

    def wide(per_column):
        return per_column[None, :, None]

    center_value = center[0]
    base_shift = jnp.min(shifts)
    delta_shift = (shifts - base_shift)[:, None]
    start = right_side
    start_image = apply_h(start)
    half_one = start_image - center_value * start
    start_norm, half_norm = lax.psum(
        jnp.stack([column_dot(start, start), column_dot(half_one, half_one)]), "rows"
    )
    alpha_one = start_norm / (half_norm + base_shift * start_norm)
    op_image = apply_h(half_one) - center_value * half_one + base_shift * start
    residual = start - wide(alpha_one) * op_image
    residual_image = apply_h(residual)
    res_norm = lax.psum(column_dot(residual, residual), "rows")
    beta_one = res_norm / start_norm
    direction = residual + wide(beta_one) * start
    half_two = residual_image - center_value * residual + wide(beta_one) * half_one
    energy = lax.psum(
        column_dot(half_two, half_two) + base_shift * column_dot(direction, direction), "rows"
    )
    from_start, from_residual = filter_factors(
        alpha_one, beta_one, res_norm / energy, delta_shift, filter_weights[:, None]
    )
    filtered = wide(from_start) * start + wide(from_residual) * residual
    applied = wide(from_start) * start_image + wide(from_residual) * residual_image
    column_piece = lax.all_gather(filtered, "cols", axis=1, tiled=True)
    correlation = jnp.einsum("iae,ibe->ab", column_piece, filtered, precision=exact_mode)
    projected = jnp.einsum("iae,ibe->ab", column_piece, applied, precision=exact_mode)
    partial_gram = jnp.stack([correlation, projected])
    summed = lax.psum(partial_gram, "rows")
    row_total = peer_count * block_rows * block_width
    return (filtered, summed[0] / row_total, summed[1] / row_total)


def split(value):
    high = value.astype(jnp.bfloat16)
    low = (value - high.astype(jnp.float32)).astype(jnp.bfloat16)
    return high, low


def lane_sum(value):
    return jnp.sum(value, axis=1, keepdims=True)


def row_sum(value):
    return jnp.sum(value, axis=0, keepdims=True)


def filter_kernel(n_rows, n_cols, groups, *refs):
    (
        blocks_hbm,
        cols_hbm,
        vec_hbm,
        center_ref,
        shifts_hbm,
        weights_hbm,
        out_ref,
        gram_ref,
        ritz_ref,
        *scratch,
    ) = refs
    block_rows, vecs, width = out_ref.shape
    per_row = blocks_hbm.shape[1]
    row_blocks, scratch = scratch[:block_rows], scratch[block_rows:]
    (
        cols_vmem,
        vec_ref,
        shifts_vmem,
        weights_vmem,
        high,
        low,
        running,
        index_vmem,
        mask_vmem,
        index_smem,
        mask_smem,
        lists_send,
        lists,
        vec_send,
        vec_recv,
        prod_send,
        prod_recv,
        col_start,
        col_image,
        image_send,
        sums_send,
        sums_recv,
        known_send,
        known_recv,
        early_send,
        early_recv,
        middle_send,
        middle_recv,
        last_send,
        last_recv,
        energy_send,
        energy_recv,
        load_sems,
        small_sems,
        list_sems,
        vec_sems,
        prod_sems,
        col_sems,
        sums_sems,
        early_sems,
        middle_sems,
        last_sems,
        energy_sems,
    ) = scratch
    far = per_row - block_rows
    mine = block_rows * width
    pair = CAP * width
    peers = n_rows - 1
    slots = CAP * peers
    share = vecs // groups
    me = lax.axis_index("rows")
    me_col = lax.axis_index("cols")
    pending = []

    smalls = [
        pltpu.make_async_copy(src, dst, small_sems.at[i])
        for i, (src, dst) in enumerate(
            [
                (cols_hbm, cols_vmem),
                (vec_hbm, vec_ref),
                (shifts_hbm, shifts_vmem),
                (weights_hbm, weights_vmem),
            ]
        )
    ]
    for copy in smalls:
        copy.start()
    loads = [
        pltpu.make_async_copy(blocks_hbm.at[row], row_blocks[row], load_sems.at[row])
        for row in range(block_rows)
    ]
    for copy in loads:
        copy.start()

    barrier = pltpu.get_barrier_semaphore()
    for step in range(1, n_rows):
        pl.semaphore_signal(barrier, inc=1, device_id={"rows": lax.rem(me + step, n_rows)})
    for step in range(1, n_cols):
        pl.semaphore_signal(barrier, inc=1, device_id={"cols": lax.rem(me_col + step, n_cols)})

    def begin(src, dst, send, recv, where):
        copy = pltpu.make_async_remote_copy(
            src_ref=src,
            dst_ref=dst,
            send_sem=send,
            recv_sem=recv,
            device_id=where,
            device_id_type=pl.DeviceIdType.MESH,
        )
        copy.start()
        pending.append(copy)
        return copy

    def to_row(src, dst, sems, step):
        where = {"rows": lax.rem(me + step, n_rows)}
        return begin(src, dst, sems.at[0, step - 1], sems.at[1, peers - step], where)

    def to_col(src, dst, sems, step):
        where = {"cols": lax.rem(me_col + step, n_cols)}
        return begin(src, dst, sems.at[0, step - 1], sems.at[1, n_cols - 1 - step], where)

    def arrive(copies):
        for copy in copies:
            copy.wait_recv()

    def place_blocks():
        columns = cols_vmem[...]
        place = lax.broadcasted_iota(jnp.int32, columns.shape, 1)
        lane = lax.broadcasted_iota(jnp.int32, (block_rows, width), 1)
        own = columns - me * block_rows
        slot = jnp.full(columns.shape, -1, jnp.int32)
        for step in range(1, n_rows):
            inner = columns - lax.rem(me + step, n_rows) * block_rows
            hit = (place >= block_rows) & (inner >= 0) & (inner < block_rows)
            value = inner.astype(jnp.float32)
            first = jnp.where(hit, value, float(block_rows))
            first = jnp.min(jnp.min(first, axis=1, keepdims=True), axis=0, keepdims=True)
            last = jnp.where(hit, value, -1.0)
            last = jnp.max(jnp.max(last, axis=1, keepdims=True), axis=0, keepdims=True)
            upper = (inner == last.astype(jnp.int32)).astype(jnp.int32)
            slot = jnp.where(hit, CAP * (step - 1) + upper, slot)
            lists_send[step - 1, 0:1, :] = jnp.broadcast_to(first, (1, width))
            lists_send[step - 1, 1:2, :] = jnp.broadcast_to(last, (1, width))
        key = slot * per_row + place
        rank = jnp.zeros(columns.shape, jnp.int32)
        follows = jnp.zeros(columns.shape, jnp.int32)
        for k in range(block_rows, per_row):
            rank = rank + (key[:, k : k + 1] < key).astype(jnp.int32)
            same = (slot[:, k : k + 1] == slot) & (place > k)
            follows = follows | same.astype(jnp.int32)
        order = jnp.zeros(lane.shape, jnp.int32)
        keep = jnp.zeros(lane.shape, jnp.int32)
        ends = jnp.full(lane.shape, -1, jnp.int32)
        live = jnp.zeros(lane.shape, jnp.int32)
        for k in range(block_rows):
            order = order + jnp.where(own[:, k : k + 1] == lane, k, 0)
        for k in range(block_rows, per_row):
            here = rank[:, k : k + 1] == lane - block_rows
            order = order + jnp.where(here, k, 0)
            keep = keep + jnp.where(here, follows[:, k : k + 1], 0)
            ends = ends + (slot[:, k : k + 1] <= lane - per_row).astype(jnp.int32)
            live = live | (slot[:, k : k + 1] == lane - per_row).astype(jnp.int32)
        tail = lane >= per_row
        ends = jnp.minimum(jnp.maximum(ends, 0), far - 1)
        index_vmem[...] = jnp.where(tail, ends, jnp.minimum(order, per_row - 1))
        mask_vmem[...] = jnp.where(tail, live, keep).astype(jnp.float32)
        moves = [
            pltpu.make_async_copy(index_vmem, index_smem, small_sems.at[4]),
            pltpu.make_async_copy(mask_vmem, mask_smem, small_sems.at[5]),
        ]
        for move in moves:
            move.start()
        return moves

    smalls[0].wait()
    moves = place_blocks()
    pl.semaphore_wait(barrier, peers + n_cols - 1)
    list_copies = [
        to_row(lists_send.at[step - 1], lists.at[peers - step], list_sems, step)
        for step in range(1, n_rows)
    ]
    for copy in smalls[1:]:
        copy.wait()
    col_start[me_col] = vec_ref[...]
    start_copies = [
        to_col(vec_ref, col_start.at[me_col], col_sems.at[0], step) for step in range(1, n_cols)
    ]
    for move in moves:
        move.wait()

    chunk = running.shape[1]
    for row in range(block_rows):
        loads[row].wait()
        source = row_blocks[row]

        @pl.loop(0, width // chunk)
        def _(part):
            lines = pl.ds(pl.multiple_of(part * chunk, chunk), chunk)
            target = pl.ds(pl.multiple_of(row * width + part * chunk, chunk), chunk)

            def put(spot, value):
                top, bottom = split(value)
                high[spot, target, :] = top
                low[spot, target, :] = bottom

            total = jnp.zeros((chunk, width), jnp.float32)
            for j in range(far):
                block = source[index_smem[row, block_rows + j], lines, :]
                total = total * mask_smem[row, block_rows + j] + block
                running[j] = total
            for spot in range(block_rows):
                put(spot, source[index_smem[row, spot], lines, :])
            for s in range(slots):
                value = running[index_smem[row, per_row + s]] * mask_smem[row, per_row + s]
                put(block_rows + s, value)

    def flat(ref):
        return jnp.concatenate([ref[i] for i in range(block_rows)], axis=1)

    def named(step, slot, row):
        return jnp.broadcast_to(lists[step - 1, slot : slot + 1, :], (share, width)) == float(row)

    def dot(a, b, transposed):
        return lax.dot_general(
            a, b, (((1,), (1 if transposed else 0,)), ((), ())),
            preferred_element_type=jnp.float32,
        )

    def stacked(value):
        top, bottom = split(value)
        return top, jnp.concatenate([top, bottom], axis=0)

    def times(parts, rhs_high, rhs_low, transposed):
        top, both = parts
        wide_part = dot(both, rhs_high, transposed)
        count = top.shape[0]
        return wide_part[:count] + wide_part[count:] + dot(top, rhs_low, transposed)

    def columns(ref, first, count):
        return jnp.concatenate([ref[first + k] for k in range(count)], axis=1)

    def near(parts, transposed):
        return times(
            parts, columns(high, 0, block_rows), columns(low, 0, block_rows), transposed
        )

    def remote(parts, step, transposed):
        first = block_rows + CAP * (step - 1)
        return times(parts, columns(high, first, CAP), columns(low, first, CAP), transposed)

    sub_lane = lax.broadcasted_iota(jnp.int32, (share, width), 1)
    sub_row = lax.broadcasted_iota(jnp.int32, (share, width), 0)

    def as_row(value, first):
        spread = jnp.where(sub_lane == sub_row + first, value, 0.0)
        return row_sum(spread)

    def as_column(row_value, first):
        spread = jnp.where(sub_lane == sub_row + first, row_value, 0.0)
        return lane_sum(spread)

    def send_sums(turn, g, values):
        packed = as_row(values[0], 0)
        for q, value in enumerate(values[1:]):
            packed = packed + as_row(value, (q + 1) * share)
        sums_send[turn, g] = packed
        return [
            to_row(
                sums_send.at[turn, g],
                sums_recv.at[turn, g, peers - step],
                sums_sems.at[turn, g],
                step,
            )
            for step in range(1, n_rows)
        ]

    def total_sums(turn, g, copies, count):
        arrive(copies)
        total = sums_send[turn, g]
        for step in range(1, n_rows):
            total = total + sums_recv[turn, g, step - 1]
        return [as_column(total, q * share) for q in range(count)]

    def send_vectors(turn, g, vector):
        copies = []
        for step in range(1, n_rows):
            for slot in range(CAP):
                picked = jnp.zeros((share, width), jnp.float32)
                for row in range(block_rows):
                    piece = vector[:, row * width : (row + 1) * width]
                    picked = jnp.where(named(step, slot, row), piece, picked)
                vec_send[turn, g, step - 1, :, slot * width : (slot + 1) * width] = picked
            copies.append(
                to_row(
                    vec_send.at[turn, g, step - 1],
                    vec_recv.at[turn, g, peers - step],
                    vec_sems.at[turn, g],
                    step,
                )
            )
        return copies

    def send_products(turn, g, parts):
        copies = []
        for step in range(1, n_rows):
            prod_send[turn, g, step - 1] = remote(parts, step, False)
            copies.append(
                to_row(
                    prod_send.at[turn, g, step - 1],
                    prod_recv.at[turn, g, peers - step],
                    prod_sems.at[turn, g],
                    step,
                )
            )
        return copies

    def collect(turn, g, result, vectors, products):
        for step in range(1, n_rows):
            vectors[peers - step].wait_recv()
            result = result + remote(stacked(vec_recv[turn, g, step - 1]), step, True)
        pieces = [result[:, row * width : (row + 1) * width] for row in range(block_rows)]
        for step in range(1, n_rows):
            products[peers - step].wait_recv()
            for slot in range(CAP):
                back = prod_recv[turn, g, step - 1, :, slot * width : (slot + 1) * width]
                for row in range(block_rows):
                    pieces[row] = pieces[row] + jnp.where(named(step, slot, row), back, 0.0)
        return jnp.concatenate(pieces, axis=1)

    def local(parts):
        return near(parts, False) + near(parts, True)

    every_group = range(groups)
    center = center_ref[0]
    base = jnp.min(shifts_vmem[...], axis=1, keepdims=True)

    def take(g):
        return slice(g * share, (g + 1) * share)

    start = [
        jnp.concatenate([vec_ref[i, take(g), :] for i in range(block_rows)], axis=1)
        for g in every_group
    ]

    parts = [stacked(start[g]) for g in every_group]
    products = [send_products(0, g, parts[g]) for g in every_group]
    arrive(list_copies)
    vectors = [send_vectors(0, g, start[g]) for g in every_group]
    results = [local(parts[g]) for g in every_group]
    arrive(start_copies)

    def gathered(ref):
        return split(jnp.concatenate([flat(ref.at[c]) for c in range(n_cols)], axis=0))

    every_start = gathered(col_start)

    image, half, sum_copies = [], [], []
    next_parts, next_products, next_vectors, next_results = [], [], [], []
    for g in every_group:
        image.append(collect(0, g, results[g], vectors[g], products[g]))
        half.append(image[g] - center * start[g])
        next_vectors.append(send_vectors(1, g, half[g]))
        next_parts.append(stacked(half[g]))
        next_products.append(send_products(1, g, next_parts[g]))
        own = [lane_sum(start[g] * start[g]), lane_sum(half[g] * half[g])]
        sum_copies.append(send_sums(0, g, own))
        next_results.append(local(next_parts[g]))

    def whole(pieces):
        return jnp.concatenate(pieces, axis=0)

    def send_all(src, dst, sems):
        return [
            to_row(src, dst.at[peers - step], sems, step) for step in range(1, n_rows)
        ]

    count = n_cols * vecs
    early = times(stacked(jnp.concatenate([whole(start), whole(image)], axis=0)), *every_start, True)
    early_send[...] = jnp.concatenate([early[:vecs], early[vecs:]], axis=1)
    early_copies = send_all(early_send, early_recv, early_sems)

    second, residual, alpha, start_norm, norm_copies = [], [], [], [], []
    parts, products, vectors, results = [], [], [], []
    for g in every_group:
        applied = collect(1, g, next_results[g], next_vectors[g], next_products[g])
        second.append(applied - center * half[g])
        norm_one, half_norm = total_sums(0, g, sum_copies[g], 2)
        start_norm.append(norm_one)
        alpha.append(norm_one / (half_norm + base * norm_one))
        residual.append(start[g] - alpha[g] * (second[g] + base * start[g]))
        vectors.append(send_vectors(2, g, residual[g]))
        parts.append(stacked(residual[g]))
        products.append(send_products(2, g, parts[g]))
        norm_copies.append(send_sums(1, g, [lane_sum(residual[g] * residual[g])]))
        for row in range(block_rows):
            image_send[row, take(g), :] = second[g][:, row * width : (row + 1) * width]
    col_image[me_col] = image_send[...]
    image_copies = [
        to_col(image_send, col_image.at[me_col], col_sems.at[1], step)
        for step in range(1, n_cols)
    ]
    results = [local(parts[g]) for g in every_group]

    arrive(image_copies)
    every_image = gathered(col_image)
    middle = times(
        stacked(jnp.concatenate([whole(start), whole(image), whole(second)], axis=0)),
        *every_image,
        True,
    )
    half_vecs = vecs // 2
    middle_send[:vecs] = jnp.concatenate([middle[:vecs], middle[vecs : 2 * vecs]], axis=1)
    middle_send[vecs:] = jnp.concatenate(
        [middle[2 * vecs : 2 * vecs + half_vecs], middle[2 * vecs + half_vecs :]], axis=1
    )
    middle_copies = send_all(middle_send, middle_recv, middle_sems)

    final_image, beta, res_norm = [], [], []
    known = None
    for g in every_group:
        final_image.append(collect(2, g, results[g], vectors[g], products[g]))
        (norm_two,) = total_sums(1, g, norm_copies[g], 1)
        res_norm.append(norm_two)
        beta.append(norm_two / start_norm[g])
    spot = me_col * vecs
    energy = None
    for g in every_group:
        direction = residual[g] + beta[g] * start[g]
        half_two = final_image[g] - center * residual[g] + beta[g] * half[g]
        own = lane_sum(half_two * half_two + base * (direction * direction))
        row_value = as_row(own, spot + g * share)
        energy = row_value if energy is None else energy + row_value
    energy_send[...] = energy
    energy_copies = []
    for row_step in range(n_rows):
        for col_step in range(n_cols):
            if row_step == 0 and col_step == 0:
                continue
            number = row_step * n_cols + col_step - 1
            opposite = ((n_rows - row_step) % n_rows) * n_cols + (n_cols - col_step) % n_cols - 1
            energy_copies.append(
                begin(
                    energy_send,
                    energy_recv.at[opposite],
                    energy_sems.at[0, number],
                    energy_sems.at[1, opposite],
                    {
                        "rows": lax.rem(me + row_step, n_rows),
                        "cols": lax.rem(me_col + col_step, n_cols),
                    },
                )
            )
    last = times(stacked(whole(final_image)), *every_image, True)
    last_send[...] = jnp.concatenate([last[:half_vecs], last[half_vecs:]], axis=1)
    last_copies = send_all(last_send, last_recv, last_sems)

    def known_row(values):
        total = None
        for g in every_group:
            row_value = as_row(values[g], spot + g * share)
            total = row_value if total is None else total + row_value
        return total

    known = [known_row(alpha), known_row(beta), known_row(res_norm)]
    known_send[...] = jnp.concatenate(
        known + [jnp.zeros((8 - len(known), width), jnp.float32)], axis=0
    )
    known_copies = [
        to_col(known_send, known_recv.at[step - 1], col_sems.at[2], n_cols - step)
        for step in range(1, n_cols)
    ]

    def summed(own_ref, recv, copies):
        arrive(copies)
        total = own_ref[...]
        for step in range(1, n_rows):
            total = total + recv[step - 1]
        return total

    early_total = summed(early_send, early_recv, early_copies)
    middle_total = summed(middle_send, middle_recv, middle_copies)
    arrive(known_copies)
    shared = known_send[...]
    for step in range(1, n_cols):
        shared = shared + known_recv[step - 1]
    live = lax.broadcasted_iota(jnp.int32, (1, width), 1) < count
    alpha_one, beta_one, norm_two = [
        jnp.where(live, shared[q : q + 1], 1.0) for q in range(3)
    ]
    arrive(energy_copies)
    total_energy = energy_send[...]
    for number in range(n_rows * n_cols - 1):
        total_energy = total_energy + energy_recv[number]
    alpha_two = norm_two / jnp.where(live, total_energy, 1.0)
    from_start = jnp.zeros((1, width), jnp.float32)
    from_residual = from_start
    for m in range(shifts_vmem.shape[1]):
        delta = shifts_vmem[:, m : m + 1] - base
        weight = weights_vmem[:, m : m + 1]
        zeta_one = 1.0 / (1.0 + delta * alpha_one)
        zeta_two = (
            zeta_one
            * alpha_one
            / (
                alpha_two * beta_one * (1.0 - zeta_one)
                + alpha_one * (1.0 + delta * alpha_two)
            )
        )
        from_start = from_start + weight * (
            alpha_one * zeta_one + alpha_two * beta_one * zeta_one * zeta_two
        )
        from_residual = from_residual + weight * (alpha_two * zeta_two)
    on_start = from_start + from_residual * (1.0 - alpha_one * base)
    on_image = -from_residual * alpha_one

    def own_column(row_value):
        return whole([as_column(row_value, spot + g * share) for g in every_group])

    for g in every_group:
        along_start = as_column(from_start, spot + g * share)
        along_residual = as_column(from_residual, spot + g * share)
        filtered = along_start * start[g] + along_residual * residual[g]
        for row in range(block_rows):
            out_ref[row, take(g), :] = filtered[:, row * width : (row + 1) * width]
    start_b, image_b = own_column(on_start), own_column(on_image)
    first_b, residual_b = own_column(from_start), own_column(from_residual)
    start_a, image_a = on_start[:, :count], on_image[:, :count]
    last_total = summed(last_send, last_recv, last_copies)
    squares = jnp.concatenate([middle_total[vecs:, :count], middle_total[vecs:, count:]], axis=0)
    closing = jnp.concatenate([last_total[:, :count], last_total[:, count:]], axis=0)
    scale = 1.0 / (n_rows * mine)
    gram_ref[...] = scale * (
        start_b * start_a * early_total[:, :count]
        + (start_b * image_a + image_b * start_a) * middle_total[:vecs, :count]
        + image_b * image_a * squares
    )
    ritz_ref[...] = scale * (
        start_b * start_a * early_total[:, count:]
        + (first_b * image_a + image_b * start_a) * middle_total[:vecs, count:]
        + residual_b * image_a * closing
    )
    for copy in pending:
        copy.wait_send()


def deliver_kernel(*refs):
    sems = refs[-1]
    half = (len(refs) - 1) // 2
    copies = [
        pltpu.make_async_copy(refs[i], refs[half + i], sems.at[i]) for i in range(half)
    ]
    for copy in copies:
        copy.start()
    for copy in copies:
        copy.wait()


def deliver(arrays):
    return pl.pallas_call(
        deliver_kernel,
        out_shape=[jax.ShapeDtypeStruct(a.shape, a.dtype) for a in arrays],
        in_specs=[pl.BlockSpec(memory_space=pltpu.VMEM)] * len(arrays),
        out_specs=[pl.BlockSpec(memory_space=pltpu.HBM)] * len(arrays),
        scratch_shapes=[pltpu.SemaphoreType.DMA((len(arrays),))],
        compiler_params=pltpu.CompilerParams(vmem_limit_bytes=1 << 20),
    )(*arrays)


def in_hbm(value):
    return pltpu.with_memory_space_constraint(value, pltpu.HBM)


GROUPS = 1


def fused_shards(
    n_rows, n_cols, hblocks, col_index, right_side, center, shifts, filter_weights
):
    block_rows, per_row, width, _ = hblocks.shape
    vecs = right_side.shape[1]
    peers = n_rows - 1
    slots = CAP * peers
    far = per_row - block_rows
    mine = block_rows * width
    columns = n_cols * vecs
    pair = CAP * width
    groups = GROUPS
    share = vecs // groups
    chunk = 32
    vmem = pl.BlockSpec(memory_space=pltpu.VMEM)
    hbm = pl.BlockSpec(memory_space=pltpu.HBM)
    f32 = jnp.float32
    exchange = pltpu.VMEM((3, groups, peers, share, pair), f32)
    packed = pltpu.VMEM((block_rows + slots, mine, width), jnp.bfloat16)
    all_but_me = n_rows * n_cols - 1
    outputs = pl.pallas_call(
        functools.partial(filter_kernel, n_rows, n_cols, groups),
        out_shape=[
            jax.ShapeDtypeStruct(right_side.shape, f32),
            jax.ShapeDtypeStruct((vecs, columns), f32),
            jax.ShapeDtypeStruct((vecs, columns), f32),
        ],
        in_specs=[hbm, hbm, hbm, pl.BlockSpec(memory_space=pltpu.SMEM), hbm, hbm],
        out_specs=[vmem, vmem, vmem],
        scratch_shapes=[pltpu.VMEM((per_row, width, width), f32)] * block_rows
        + [
            pltpu.VMEM(col_index.shape, jnp.int32),
            pltpu.VMEM(right_side.shape, f32),
            pltpu.VMEM((1, shifts.shape[0]), f32),
            pltpu.VMEM((1, shifts.shape[0]), f32),
            packed,
            packed,
            pltpu.VMEM((far, chunk, width), f32),
            pltpu.VMEM((block_rows, width), jnp.int32),
            pltpu.VMEM((block_rows, width), f32),
            pltpu.SMEM((block_rows, width), jnp.int32),
            pltpu.SMEM((block_rows, width), f32),
            pltpu.VMEM((peers, CAP, width), f32),
            pltpu.VMEM((peers, CAP, width), f32),
            exchange,
            exchange,
            exchange,
            exchange,
            pltpu.VMEM((n_cols,) + right_side.shape, f32),
            pltpu.VMEM((n_cols,) + right_side.shape, f32),
            pltpu.VMEM(right_side.shape, f32),
            pltpu.VMEM((2, groups, 1, width), f32),
            pltpu.VMEM((2, groups, peers, 1, width), f32),
            pltpu.VMEM((8, width), f32),
            pltpu.VMEM((n_cols - 1, 8, width), f32),
            pltpu.VMEM((vecs, 2 * columns), f32),
            pltpu.VMEM((peers, vecs, 2 * columns), f32),
            pltpu.VMEM((vecs + vecs // 2, 2 * columns), f32),
            pltpu.VMEM((peers, vecs + vecs // 2, 2 * columns), f32),
            pltpu.VMEM((vecs // 2, 2 * columns), f32),
            pltpu.VMEM((peers, vecs // 2, 2 * columns), f32),
            pltpu.VMEM((1, width), f32),
            pltpu.VMEM((all_but_me, 1, width), f32),
            pltpu.SemaphoreType.DMA((block_rows,)),
            pltpu.SemaphoreType.DMA((6,)),
            pltpu.SemaphoreType.DMA((2, peers)),
            pltpu.SemaphoreType.DMA((3, groups, 2, peers)),
            pltpu.SemaphoreType.DMA((3, groups, 2, peers)),
            pltpu.SemaphoreType.DMA((3, 2, n_cols - 1)),
            pltpu.SemaphoreType.DMA((2, groups, 2, peers)),
            pltpu.SemaphoreType.DMA((2, peers)),
            pltpu.SemaphoreType.DMA((2, peers)),
            pltpu.SemaphoreType.DMA((2, peers)),
            pltpu.SemaphoreType.DMA((2, all_but_me)),
        ],
        compiler_params=pltpu.CompilerParams(
            collective_id=0, has_side_effects=True, vmem_limit_bytes=48 << 20
        ),
    )(
        in_hbm(hblocks),
        in_hbm(col_index),
        in_hbm(right_side),
        center,
        in_hbm(shifts.reshape(1, -1)),
        in_hbm(filter_weights.reshape(1, -1)),
    )
    filtered, gram, ritz = deliver(outputs)
    return filtered, gram.T, ritz.T


def solution(mesh):
    placed = (P("rows", None, None, None), P("rows", None), P("rows", "cols", None), P(), P(), P())
    n_rows, n_cols = mesh.shape["rows"], mesh.shape["cols"]

    def body(hblocks, col_index, right_side, *rest):
        block_rows, per_row, width = hblocks.shape[:3]
        vecs = right_side.shape[1]
        peers = n_rows - 1
        fits = (
            CAP * peers * block_rows <= block_rows * per_row
            and per_row + CAP * peers <= width
            and 2 * n_cols * vecs == width
            and vecs % (8 * GROUPS) == 0
            and vecs % 16 == 0
        )
        if fits:
            return fused_shards(n_rows, n_cols, hblocks, col_index, right_side, *rest)
        return shards(hblocks, col_index, right_side, *rest)

    return jax.shard_map(
        body,
        mesh=mesh,
        in_specs=placed,
        out_specs=(P("rows", "cols", None), P(None, "cols"), P(None, "cols")),
        check_vma=False,
    )
```

```python
import functools

import jax
import jax.numpy as jnp
from jax import lax
from jax.experimental import pallas as pl
from jax.experimental.pallas import tpu as pltpu
from jax.sharding import PartitionSpec as P

CAP = 2


exact_mode = lax.Precision.HIGHEST


def column_dot(first_arr, second_arr):
    return jnp.sum(first_arr * second_arr, axis=(0, 2))


def ordered_lists(need_mask, slot_width):
    ranks = jnp.cumsum(need_mask, axis=1)
    positions = lax.broadcasted_iota(jnp.int32, need_mask.shape, 1)
    columns_out = []
    for slot in range(slot_width):
        hit = (need_mask > 0) & (ranks == slot + 1)
        columns_out.append(jnp.sum(jnp.where(hit, positions, 0), axis=1))
    lists = jnp.stack(columns_out, axis=1)
    live = jnp.sum(need_mask, axis=1, keepdims=True) > 0
    return jnp.where(live, lists, -1)


def filter_factors(alpha_one, beta_one, alpha_two, delta_shift, weights):
    zeta_one = 1.0 / (1.0 + delta_shift * alpha_one)
    zeta_two = (
        zeta_one
        * alpha_one
        / (alpha_two * beta_one * (1.0 - zeta_one) + alpha_one * (1.0 + delta_shift * alpha_two))
    )
    from_start = jnp.sum(
        weights * (alpha_one * zeta_one + alpha_two * beta_one * zeta_one * zeta_two), axis=0
    )
    from_residual = jnp.sum(weights * (alpha_two * zeta_two), axis=0)
    return from_start, from_residual


def shards(hblocks, col_index, right_side, center, shifts, filter_weights):
    block_rows = hblocks.shape[0]
    block_width = hblocks.shape[2]
    local_vecs = right_side.shape[1]
    pole_count = shifts.shape[0]
    peer_count = lax.axis_size("rows")
    slot_width = CAP
    device_index = lax.axis_index("rows")
    own_cols = col_index[:, :block_rows] - device_index * block_rows
    far_cols = col_index[:, block_rows:].reshape(-1)
    near_blocks = hblocks[:, :block_rows]
    far_blocks = hblocks[:, block_rows:]
    every_key = jnp.arange(peer_count * block_rows, dtype=jnp.int32)
    need_mask = (
        jnp.any(far_cols[:, None] == every_key[None, :], axis=0)
        .astype(jnp.int32)
        .reshape(peer_count, block_rows)
    )
    incoming_mask = lax.all_to_all(need_mask, "rows", split_axis=0, concat_axis=0, tiled=True)
    send_lists = ordered_lists(incoming_mask, slot_width)
    my_lists = ordered_lists(need_mask, slot_width)
    owners = lax.broadcasted_iota(jnp.int32, my_lists.shape, 0)
    slot_keys = jnp.where(my_lists >= 0, owners * block_rows + my_lists, -1).reshape(-1)
    slot_total = slot_keys.shape[0]
    matches = far_cols[:, None] == slot_keys[None, :]
    picker = matches.astype(jnp.float32)
    slot_numbers = lax.broadcasted_iota(jnp.int32, matches.shape, 1)
    slot_of_ref = jnp.sum(jnp.where(matches, slot_numbers, 0), axis=1)
    row_numbers = jnp.arange(block_rows, dtype=jnp.int32)[:, None]
    spread = (send_lists.reshape(-1)[None, :] == row_numbers).astype(jnp.float32)
    own_spread = (own_cols.reshape(-1)[None, :] == row_numbers).astype(jnp.float32)
    send_index = jnp.maximum(send_lists, 0)
    send_live = (send_lists >= 0)[:, :, None, None]

    def apply_h(vector):
        far_terms = jnp.einsum("ikab,iva->ikvb", far_blocks, vector, precision=exact_mode).reshape(
            far_cols.shape[0], -1
        )
        slot_sums = jnp.dot(picker.T, far_terms, precision=exact_mode).reshape(
            peer_count, slot_width, local_vecs, block_width
        )
        picked = vector[send_index]
        outgoing = jnp.where(send_live, picked, jnp.zeros_like(picked))
        both = lax.all_to_all(
            jnp.concatenate([outgoing, slot_sums], axis=1),
            "rows",
            split_axis=0,
            concat_axis=0,
            tiled=True,
        )
        arrived = both[:, :slot_width].reshape(slot_total, local_vecs, block_width)
        returned = both[:, slot_width:].reshape(slot_total, -1)
        near_vec = vector[own_cols]
        result = jnp.einsum("ikab,ikvb->iva", near_blocks, near_vec, precision=exact_mode)
        near_terms = jnp.einsum(
            "ikab,iva->ikvb", near_blocks, vector, precision=exact_mode
        ).reshape(block_rows * block_rows, -1)
        result = result + jnp.dot(own_spread, near_terms, precision=exact_mode).reshape(
            vector.shape
        )
        far_vec = arrived[slot_of_ref]
        far_vec = far_vec.reshape(block_rows, -1, local_vecs, block_width)
        result = result + jnp.einsum("ikab,ikvb->iva", far_blocks, far_vec, precision=exact_mode)
        return result + jnp.dot(spread, returned, precision=exact_mode).reshape(vector.shape)

    def wide(per_column):
        return per_column[None, :, None]

    center_value = center[0]
    base_shift = jnp.min(shifts)
    delta_shift = (shifts - base_shift)[:, None]
    start = right_side
    start_image = apply_h(start)
    half_one = start_image - center_value * start
    start_norm, half_norm = lax.psum(
        jnp.stack([column_dot(start, start), column_dot(half_one, half_one)]), "rows"
    )
    alpha_one = start_norm / (half_norm + base_shift * start_norm)
    op_image = apply_h(half_one) - center_value * half_one + base_shift * start
    residual = start - wide(alpha_one) * op_image
    residual_image = apply_h(residual)
    res_norm = lax.psum(column_dot(residual, residual), "rows")
    beta_one = res_norm / start_norm
    direction = residual + wide(beta_one) * start
    half_two = residual_image - center_value * residual + wide(beta_one) * half_one
    energy = lax.psum(
        column_dot(half_two, half_two) + base_shift * column_dot(direction, direction), "rows"
    )
    from_start, from_residual = filter_factors(
        alpha_one, beta_one, res_norm / energy, delta_shift, filter_weights[:, None]
    )
    filtered = wide(from_start) * start + wide(from_residual) * residual
    applied = wide(from_start) * start_image + wide(from_residual) * residual_image
    column_piece = lax.all_gather(filtered, "cols", axis=1, tiled=True)
    correlation = jnp.einsum("iae,ibe->ab", column_piece, filtered, precision=exact_mode)
    projected = jnp.einsum("iae,ibe->ab", column_piece, applied, precision=exact_mode)
    partial_gram = jnp.stack([correlation, projected])
    summed = lax.psum(partial_gram, "rows")
    row_total = peer_count * block_rows * block_width
    return (filtered, summed[0] / row_total, summed[1] / row_total)


def split(value):
    high = value.astype(jnp.bfloat16)
    low = (value - high.astype(jnp.float32)).astype(jnp.bfloat16)
    return high, low


def lane_sum(value):
    return jnp.sum(value, axis=1, keepdims=True)


def row_sum(value):
    return jnp.sum(value, axis=0, keepdims=True)


HALF_GAP = 32
SPOT_GAP = 16


def filter_kernel(n_rows, n_cols, refs, accumulators):
    (
        blocks_hbm,
        cols_hbm,
        vec_hbm,
        center_ref,
        shifts_hbm,
        weights_hbm,
        out_ref,
        gram_ref,
        ritz_ref,
        *scratch,
    ) = refs
    block_rows, vecs, width = out_ref.shape
    per_row = blocks_hbm.shape[1]
    row_blocks, scratch = scratch[:block_rows], scratch[block_rows:]
    (
        cols_vmem,
        vec_ref,
        shifts_vmem,
        weights_vmem,
        high,
        low,
        running,
        index_vmem,
        mask_vmem,
        index_smem,
        mask_smem,
        lists_send,
        lists,
        vec_send,
        vec_recv,
        prod_send,
        prod_recv,
        col_start,
        col_image,
        col_second,
        image_send,
        sums_send,
        sums_recv,
        known_send,
        known_recv,
        early_send,
        early_recv,
        early_half,
        early_other,
        middle_send,
        middle_recv,
        middle_half,
        middle_other,
        square_send,
        square_recv,
        last_send,
        last_recv,
        energy_send,
        energy_recv,
        load_sems,
        small_sems,
        vec_sems,
        send_sems,
        recv_sems,
    ) = scratch
    totals, terms, grams = accumulators
    far = per_row - block_rows
    mine = block_rows * width
    peers = n_rows - 1
    slots = CAP * peers
    near_peers = n_rows // 2
    count = n_cols * vecs
    me = lax.axis_index("rows")
    me_col = lax.axis_index("cols")
    drains = []
    used = [0]

    smalls = [
        pltpu.make_async_copy(src, dst, small_sems.at[i])
        for i, (src, dst) in enumerate(
            [
                (cols_hbm, cols_vmem),
                (vec_hbm, vec_ref),
                (shifts_hbm, shifts_vmem),
                (weights_hbm, weights_vmem),
            ]
        )
    ]
    smalls[0].start()
    loads = [
        pltpu.make_async_copy(blocks_hbm.at[row], row_blocks[row], load_sems.at[row])
        for row in range(block_rows)
    ]
    barrier = pltpu.get_barrier_semaphore()
    for step in range(1, n_rows):
        pl.semaphore_signal(barrier, inc=1, device_id={"rows": lax.rem(me + step, n_rows)})
    for step in range(1, n_cols):
        pl.semaphore_signal(barrier, inc=1, device_id={"cols": lax.rem(me_col + step, n_cols)})

    def begin(src, dst, send, recv, where):
        pltpu.make_async_remote_copy(
            src_ref=src,
            dst_ref=dst,
            send_sem=send,
            recv_sem=recv,
            device_id=where,
            device_id_type=pl.DeviceIdType.MESH,
        ).start()

    def row_at(step):
        return {"rows": lax.rem(me + step, n_rows)}

    def col_at(step):
        return {"cols": lax.rem(me_col + step, n_cols)}

    def bytes_of(ref, sem):
        return pltpu.make_async_copy(ref, ref, sem)

    def group(size):
        number = used[0]
        used[0] += 1
        send, recv = send_sems.at[number], recv_sems.at[number]
        drains.append(bytes_of(size, send))
        return send, recv, bytes_of(size, recv)

    def to_all(source, recv_ref):
        send, recv, landed = group(recv_ref)
        for step in range(1, n_rows):
            begin(source(step), recv_ref.at[peers - step], send, recv, row_at(step))
        return landed

    def to_cols(source, recv_ref):
        send, recv, landed = group(recv_ref)
        for step in range(1, n_cols):
            begin(source, recv_ref.at[n_cols - 1 - step], send, recv, col_at(step))
        return landed

    smalls[0].wait()
    for copy in loads + smalls[1:]:
        copy.start()
    columns = cols_vmem[...]
    place = lax.broadcasted_iota(jnp.int32, columns.shape, 1)
    is_far = place >= block_rows
    inside = []
    for step in range(1, n_rows):
        inner = columns - lax.rem(me + step, n_rows) * block_rows
        hit = is_far & (inner >= 0) & (inner < block_rows)
        value = inner.astype(jnp.float32)
        first = jnp.min(jnp.where(hit, value, float(block_rows)), axis=0, keepdims=True)
        first = jnp.min(first, axis=1, keepdims=True)
        last = jnp.max(jnp.where(hit, value, -1.0), axis=0, keepdims=True)
        last = jnp.max(last, axis=1, keepdims=True)
        lists_send[step - 1, 0:1, :] = jnp.broadcast_to(first, (1, width))
        lists_send[step - 1, 1:2, :] = jnp.broadcast_to(last, (1, width))
        inside.append((hit, inner, last))
    pl.semaphore_wait(barrier, peers + n_cols - 1)
    lists_landed = to_all(lambda step: lists_send.at[step - 1], lists)

    def place_blocks():
        lane = lax.broadcasted_iota(jnp.int32, (block_rows, width), 1)
        own = columns - me * block_rows
        slot = jnp.full(columns.shape, -1, jnp.int32)
        for number, (hit, inner, last) in enumerate(inside):
            upper = (inner == last.astype(jnp.int32)).astype(jnp.int32)
            slot = jnp.where(hit, CAP * number + upper, slot)
        key = slot * per_row + place
        rank = jnp.zeros(columns.shape, jnp.int32)
        follows = jnp.zeros(columns.shape, jnp.int32)
        for k in range(block_rows, per_row):
            rank = rank + (key[:, k : k + 1] < key).astype(jnp.int32)
            same = (slot[:, k : k + 1] == slot) & (place > k)
            follows = follows | same.astype(jnp.int32)
        order = jnp.zeros(lane.shape, jnp.int32)
        keep = jnp.zeros(lane.shape, jnp.int32)
        ends = jnp.full(lane.shape, -1, jnp.int32)
        live = jnp.zeros(lane.shape, jnp.int32)
        for k in range(block_rows):
            order = order + jnp.where(own[:, k : k + 1] == lane, k, 0)
        for k in range(block_rows, per_row):
            here = rank[:, k : k + 1] == lane - block_rows
            order = order + jnp.where(here, k, 0)
            keep = keep + jnp.where(here, follows[:, k : k + 1], 0)
            ends = ends + (slot[:, k : k + 1] <= lane - per_row).astype(jnp.int32)
            live = live | (slot[:, k : k + 1] == lane - per_row).astype(jnp.int32)
        tail = lane >= per_row
        ends = jnp.minimum(jnp.maximum(ends, 0), far - 1)
        index_vmem[...] = jnp.where(tail, ends, jnp.minimum(order, per_row - 1))
        mask_vmem[...] = jnp.where(tail, live, keep).astype(jnp.float32)
        moves = [
            pltpu.make_async_copy(index_vmem, index_smem, small_sems.at[4]),
            pltpu.make_async_copy(mask_vmem, mask_smem, small_sems.at[5]),
        ]
        for move in moves:
            move.start()
        return moves

    moves = place_blocks()
    for move in moves:
        move.wait()

    chunk = running.shape[1]
    half_rows = block_rows // 2
    for row in range(block_rows):
        loads[row].wait()
        source = row_blocks[row]
        base_line = row * width + (HALF_GAP if row >= half_rows else 0)

        @pl.loop(0, width // chunk)
        def _(part):
            lines = pl.ds(pl.multiple_of(part * chunk, chunk), chunk)
            target = pl.ds(pl.multiple_of(base_line + part * chunk, 16), chunk)

            def put(spot, value):
                top, bottom = split(value)
                high[spot, target, :] = top
                low[spot, target, :] = bottom

            total = jnp.zeros((chunk, width), jnp.float32)
            for j in range(far):
                block = source[index_smem[row, block_rows + j], lines, :]
                total = total * mask_smem[row, block_rows + j] + block
                running[j] = total
            for spot in range(block_rows):
                put(spot, source[index_smem[row, spot], lines, :])
            for s in range(slots):
                value = running[index_smem[row, per_row + s]] * mask_smem[row, per_row + s]
                put(block_rows + s, value)

    tile = 2 * width
    tiles = block_rows // 2
    staged = [0, 0]

    def feed(unit, weights, transposed, uses):
        register = staged[unit]
        staged[unit] = 1 - register
        pltpu.matmul_push_rhs(weights, register, unit, transpose=transposed)
        for number, (acc, rows) in enumerate(uses):
            pltpu.matmul_acc_lhs(acc, rows, register if number == 0 else None)

    def block(ref, spot, lines):
        begin_at = lines * tile + (HALF_GAP if lines >= tiles // 2 else 0)
        first = slice(begin_at, begin_at + tile)
        return jnp.concatenate([ref[spot, first, :], ref[spot + 1, first, :]], axis=1)

    def multiply(unit, acc, parts, spot, lines, at, transposed):
        top, bottom = [part[:, at * tile : (at + 1) * tile] for part in parts]
        feed(unit, block(high, spot, lines), transposed, [(acc, top), (acc, bottom)])
        feed(unit, block(low, spot, lines), transposed, [(acc, top)])

    half_tiles = tiles // 2

    def sum_of(n):
        return totals[n // half_tiles][n % half_tiles]

    woven = [n + u * half_tiles for n in range(half_tiles) for u in range(2)]

    def flat(ref):
        return jnp.concatenate([ref[i] for i in range(block_rows)], axis=1)

    def piece(value, row):
        return value[:, row * width : (row + 1) * width]

    def named(step, slot, row):
        return jnp.broadcast_to(lists[step - 1, slot : slot + 1, :], (vecs, width)) == float(row)

    lane_of = lax.broadcasted_iota(jnp.int32, (vecs, width), 1)
    row_of = lax.broadcasted_iota(jnp.int32, (vecs, width), 0)

    def as_row(value, first):
        return row_sum(jnp.where(lane_of == row_of + first, value, 0.0))

    def as_column(row_value, first):
        return lane_sum(jnp.where(lane_of == row_of + first, row_value, 0.0))

    def send_sums(turn, values):
        packed = as_row(values[0], 0)
        for q, value in enumerate(values[1:]):
            packed = packed + as_row(value, (q + 1) * vecs)
        sums_send[turn] = packed
        return to_all(lambda step: sums_send.at[turn], sums_recv.at[turn])

    def total_sums(turn, landed, quantities):
        landed.wait()
        total = sums_send[turn]
        for step in range(1, n_rows):
            total = total + sums_recv[turn, step - 1]
        return [as_column(total, q * vecs) for q in range(quantities)]

    def send_vectors(turn, vector):
        number = used[0]
        used[0] += 1
        send = send_sems.at[number]
        drains.append(bytes_of(vec_send.at[turn], send))
        for step in range(1, n_rows):
            for slot in range(CAP):
                picked = jnp.zeros((vecs, width), jnp.float32)
                for row in range(block_rows):
                    picked = jnp.where(named(step, slot, row), piece(vector, row), picked)
                vec_send[turn, step - 1, :, slot * width : (slot + 1) * width] = picked
            begin(
                vec_send.at[turn, step - 1],
                vec_recv.at[turn, peers - step],
                send,
                vec_sems.at[turn, peers - step],
                row_at(step),
            )

    def send_products(turn, parts):
        send, recv, landed = group(prod_recv.at[turn])

        def launch(ready):
            for step, accs in ready:
                value = functools.reduce(jnp.add, [pltpu.matmul_pop(acc) for acc in accs])
                prod_send[turn, step - 1] = value
                begin(
                    prod_send.at[turn, step - 1],
                    prod_recv.at[turn, peers - step],
                    send,
                    recv,
                    row_at(step),
                )

        ready = []
        for first in range(1, n_rows, 2):
            which = (first // 2) % 2
            even, odd = terms[0][which], terms[1][which]
            spot = block_rows + CAP * (first - 1)
            if first + 1 < n_rows:
                for lines in range(tiles):
                    multiply(0, even, parts, spot, lines, lines, False)
                    multiply(1, odd, parts, spot + CAP, lines, lines, False)
                done = [(first, [even]), (first + 1, [odd])]
            else:
                for lines in range(half_tiles):
                    later = lines + half_tiles
                    multiply(0, even, parts, spot, lines, lines, False)
                    multiply(1, odd, parts, spot, later, later, False)
                done = [(first, [even, odd])]
            launch(ready)
            ready = done
        launch(ready)
        return landed

    def local(parts):
        for at in range(tiles):
            for n in woven:
                line = (at + n // half_tiles * half_tiles) % tiles
                multiply(n // half_tiles, sum_of(n), parts, 2 * n, line, line, False)
        for at in range(tiles):
            for n in woven:
                multiply(n // half_tiles, sum_of(n), parts, 2 * at, n, at, True)

    def take_vectors(turn):
        for step in range(1, n_rows):
            bytes_of(vec_recv.at[turn, step - 1], vec_sems.at[turn, step - 1]).wait()
            parts = split(vec_recv[turn, step - 1])
            spot = block_rows + CAP * (step - 1)
            for n in woven:
                multiply(n // half_tiles, sum_of(n), parts, spot, n, 0, True)
        return [pltpu.matmul_pop(sum_of(n)) for n in range(tiles)]

    def take_products(turn, halves, landed):
        result = jnp.concatenate(halves, axis=1)
        pieces = [piece(result, row) for row in range(block_rows)]
        landed.wait()
        for step in range(1, n_rows):
            for slot in range(CAP):
                back = prod_recv[turn, step - 1, :, slot * width : (slot + 1) * width]
                for row in range(block_rows):
                    pieces[row] = pieces[row] + jnp.where(named(step, slot, row), back, 0.0)
        return jnp.concatenate(pieces, axis=1)

    def gathered(own, recv):
        start_at = me_col
        pieces = []
        for c in range(n_cols):
            total = jnp.where(start_at == c, own, 0.0)
            for step in range(1, n_cols):
                other = flat(recv.at[step - 1])
                total = jnp.where(lax.rem(start_at + step, n_cols) == c, other, total)
            pieces.append(total)
        return split(jnp.concatenate(pieces, axis=0))

    def share_columns(number, value, recv_ref):
        for row in range(block_rows):
            image_send[number, row] = piece(value, row)
        return to_cols(image_send.at[number], recv_ref)

    def against(pieces, every):
        top, bottom = split(jnp.concatenate(pieces, axis=0))
        rows = jnp.concatenate([top, bottom], axis=0)
        weights = [part for parts_of in every for part in parts_of]
        weights += [jnp.zeros_like(weights[0])] * (tile // count - len(weights))
        accs = [grams[u][len(pieces) - 1] for u in range(2)]
        for at in range(mine // tile):
            lines = slice(at * tile, (at + 1) * tile)
            tall = jnp.concatenate([weight[:, lines] for weight in weights], axis=0)
            feed(at % 2, tall, True, [(accs[at % 2], rows[:, lines])])
        both = pltpu.matmul_pop(accs[0]) + pltpu.matmul_pop(accs[1])
        half = top.shape[0]
        results = []
        for number in range(len(every)):
            at = 2 * number * count
            wide_part = both[:half, at : at + count] + both[:half, at + count : at + 2 * count]
            results.append(wide_part + both[half:, at : at + count])
        return results

    half_base = me // near_peers * near_peers

    def to_half(source, recv_ref):
        send, recv, landed = group(recv_ref)
        for step in range(1, near_peers):
            where = {"rows": half_base + lax.rem(me - half_base + step, near_peers)}
            begin(source, recv_ref.at[near_peers - 1 - step], send, recv, where)
        return landed

    def to_mirror(landed, own_ref, recv_ref, half_ref, other_ref):
        landed.wait()
        half_ref[...] = summed(own_ref, recv_ref)
        send, recv, crossed = group(other_ref)
        begin(half_ref, other_ref, send, recv, row_at(near_peers))
        return crossed

    def summed(own_ref, recv):
        total = own_ref[...]
        for number in range(recv.shape[0]):
            total = total + recv[number]
        return total

    for copy in smalls[1:]:
        copy.wait()
    center = center_ref[0]
    base = jnp.min(shifts_vmem[...], axis=1, keepdims=True)
    start = flat(vec_ref)

    lists_landed.wait()
    send_vectors(0, start)
    start_landed = to_cols(vec_ref, col_start)
    parts = split(start)
    products = send_products(0, parts)
    local(parts)
    halves = take_vectors(0)
    image = take_products(0, halves, products)

    half = image - center * start
    send_vectors(1, half)
    sums_landed = send_sums(0, [lane_sum(start * start), lane_sum(half * half)])
    image_landed = share_columns(0, image, col_image)
    parts = split(half)
    products = send_products(1, parts)
    local(parts)
    start_landed.wait()
    every_start = gathered(start, col_start)
    early = against([start, image], [every_start])[0]
    early_send[...] = jnp.concatenate([early[:vecs], early[vecs:]], axis=1)
    early_landed = to_half(early_send, early_recv)
    halves = take_vectors(1)
    start_norm, half_norm = total_sums(0, sums_landed, 2)
    alpha = start_norm / (half_norm + base * start_norm)
    applied = take_products(1, halves, products)

    second = applied - center * half
    residual = start - alpha * (second + base * start)
    send_vectors(2, residual)
    norm_landed = send_sums(1, [lane_sum(residual * residual)])
    second_landed = share_columns(1, second, col_second)
    parts = split(residual)
    products = send_products(2, parts)
    early_crossed = to_mirror(early_landed, early_send, early_recv, early_half, early_other)
    image_landed.wait()
    every_image = gathered(image, col_image)
    middle_send[...] = jnp.concatenate(against([second], [every_start, every_image]), axis=1)
    middle_landed = to_half(middle_send, middle_recv)
    local(parts)
    halves = take_vectors(2)

    half_vecs = vecs // 2

    def folded(value):
        return jnp.concatenate([value[:half_vecs], value[half_vecs:]], axis=1)

    def unfolded(value):
        return jnp.concatenate([value[:, :count], value[:, count:]], axis=0)

    (res_norm,) = total_sums(1, norm_landed, 1)
    beta = res_norm / start_norm
    direction = residual + beta * start
    rest = beta * half - center * residual
    own_base = lane_sum(base * (direction * direction))
    spot = me_col * vecs
    known = [as_row(value, spot) for value in (alpha, beta, res_norm)]
    known_send[...] = jnp.concatenate(
        known + [jnp.zeros((8 - len(known), width), jnp.float32)], axis=0
    )
    known_landed = to_cols(known_send, known_recv)
    final_image = take_products(2, halves, products)

    half_two = final_image + rest
    energy_send[...] = as_row(own_base + lane_sum(half_two * half_two), spot)
    send, recv, energy_landed = group(energy_recv)
    for row_step in range(n_rows - 1, -1, -1):
        for col_step in range(n_cols):
            if row_step == 0 and col_step == 0:
                continue
            opposite = ((n_rows - row_step) % n_rows) * n_cols + (n_cols - col_step) % n_cols - 1
            begin(
                energy_send,
                energy_recv.at[opposite],
                send,
                recv,
                {**row_at(row_step), **col_at(col_step)},
            )
    second_landed.wait()
    every_second = gathered(second, col_second)
    last_send[...] = folded(against([final_image], [every_second])[0])
    last_landed = to_all(lambda step: last_send, last_recv)
    square_send[...] = folded(against([second], [every_second])[0])
    square_landed = to_all(lambda step: square_send, square_recv)
    middle_crossed = to_mirror(middle_landed, middle_send, middle_recv, middle_half, middle_other)

    early_crossed.wait()
    early_total = early_half[...] + early_other[...]
    known_landed.wait()
    shared = summed(known_send, known_recv)
    live = lax.broadcasted_iota(jnp.int32, (1, width), 1) < count
    alpha_one, beta_one, norm_two = [
        jnp.where(live, shared[q : q + 1], 1.0) for q in range(3)
    ]
    poles = []
    for m in range(shifts_vmem.shape[1]):
        delta = shifts_vmem[:, m : m + 1] - base
        weight = weights_vmem[:, m : m + 1]
        zeta_one = 1.0 / (1.0 + delta * alpha_one)
        slope = beta_one * (1.0 - zeta_one) + alpha_one * delta
        poles.append((weight, zeta_one, slope))
    middle_crossed.wait()
    middle_total = middle_half[...] + middle_other[...]
    square_landed.wait()
    squares = unfolded(summed(square_send, square_recv))
    crossed, paired = middle_total[:, :count], middle_total[:, count:]
    plain, rayleigh = early_total[:, :count], early_total[:, count:]

    energy_landed.wait()
    alpha_two = norm_two / jnp.where(live, summed(energy_send, energy_recv), 1.0)
    from_start = jnp.zeros((1, width), jnp.float32)
    from_residual = from_start
    for weight, zeta_one, slope in poles:
        zeta_two = zeta_one * alpha_one / (alpha_one + alpha_two * slope)
        from_start = from_start + weight * (
            alpha_one * zeta_one + alpha_two * beta_one * zeta_one * zeta_two
        )
        from_residual = from_residual + weight * (alpha_two * zeta_two)
    on_start = from_start + from_residual * (1.0 - alpha_one * base)
    on_image = -from_residual * alpha_one

    first_b = as_column(from_start, spot)
    residual_b = as_column(from_residual, spot)
    start_b = first_b + residual_b * (1.0 - alpha * base)
    image_b = -residual_b * alpha
    filtered = first_b * start + residual_b * residual
    for row in range(block_rows):
        out_ref[row] = piece(filtered, row)
    start_a, image_a = on_start[:, :count], on_image[:, :count]
    scale = 1.0 / (n_rows * mine)
    gram_ref[...] = scale * (
        start_b * start_a * plain
        + (start_b * image_a + image_b * start_a) * crossed
        + image_b * image_a * squares
    )
    last_landed.wait()
    closing = unfolded(summed(last_send, last_recv))
    ritz_ref[...] = scale * (
        start_b * start_a * rayleigh
        + (first_b * image_a + image_b * start_a) * paired
        + residual_b * image_a * closing
    )
    for drain in drains:
        drain.wait()


def scoped_kernel(n_rows, n_cols, *refs):
    block_rows, vecs, width = refs[6].shape

    def accumulators(rows):
        return [
            [pltpu.ACC(unit)((count, 2 * width), jnp.float32) for count in rows]
            for unit in range(2)
        ]

    pl.run_scoped(
        lambda *accs: filter_kernel(n_rows, n_cols, refs, accs),
        accumulators([vecs] * (block_rows // 4)),
        accumulators([vecs] * 2),
        accumulators([2 * vecs * pieces for pieces in (1, 2)]),
    )


def deliver_kernel(*refs):
    sems = refs[-1]
    half = (len(refs) - 1) // 2
    copies = [
        pltpu.make_async_copy(refs[i], refs[half + i], sems.at[i]) for i in range(half)
    ]
    for copy in copies:
        copy.start()
    for copy in copies:
        copy.wait()


def deliver(arrays):
    return pl.pallas_call(
        deliver_kernel,
        out_shape=[jax.ShapeDtypeStruct(a.shape, a.dtype) for a in arrays],
        in_specs=[pl.BlockSpec(memory_space=pltpu.VMEM)] * len(arrays),
        out_specs=[pl.BlockSpec(memory_space=pltpu.HBM)] * len(arrays),
        scratch_shapes=[pltpu.SemaphoreType.DMA((len(arrays),))],
        compiler_params=pltpu.CompilerParams(vmem_limit_bytes=1 << 20),
    )(*arrays)


def in_hbm(value):
    return pltpu.with_memory_space_constraint(value, pltpu.HBM)


def fused_shards(
    n_rows, n_cols, hblocks, col_index, right_side, center, shifts, filter_weights
):
    block_rows, per_row, width, _ = hblocks.shape
    vecs = right_side.shape[1]
    peers = n_rows - 1
    near_peers = n_rows // 2
    slots = CAP * peers
    far = per_row - block_rows
    mine = block_rows * width
    columns = n_cols * vecs
    pair = CAP * width
    chunk = 32
    vmem = pl.BlockSpec(memory_space=pltpu.VMEM)
    hbm = pl.BlockSpec(memory_space=pltpu.HBM)
    f32 = jnp.float32
    exchange = pltpu.VMEM((3, peers, vecs, pair), f32)
    packed = pltpu.VMEM((block_rows + slots, mine + HALF_GAP + SPOT_GAP, width), jnp.bfloat16)
    gathers = pltpu.VMEM((n_cols - 1,) + right_side.shape, f32)
    product = pltpu.VMEM((vecs, 2 * columns), f32)
    two_stages = [
        product,
        pltpu.VMEM((near_peers - 1, vecs, 2 * columns), f32),
        product,
        product,
    ]
    folded = [
        pltpu.VMEM((vecs // 2, 2 * columns), f32),
        pltpu.VMEM((peers, vecs // 2, 2 * columns), f32),
    ]
    outputs = pl.pallas_call(
        functools.partial(scoped_kernel, n_rows, n_cols),
        out_shape=[
            jax.ShapeDtypeStruct(right_side.shape, f32),
            jax.ShapeDtypeStruct((vecs, columns), f32),
            jax.ShapeDtypeStruct((vecs, columns), f32),
        ],
        in_specs=[hbm, hbm, hbm, pl.BlockSpec(memory_space=pltpu.SMEM), hbm, hbm],
        out_specs=[vmem, vmem, vmem],
        scratch_shapes=[pltpu.VMEM((per_row, width, width), f32)] * block_rows
        + [
            pltpu.VMEM(col_index.shape, jnp.int32),
            pltpu.VMEM(right_side.shape, f32),
            pltpu.VMEM((1, shifts.shape[0]), f32),
            pltpu.VMEM((1, shifts.shape[0]), f32),
            packed,
            packed,
            pltpu.VMEM((far, chunk, width), f32),
            pltpu.VMEM((block_rows, width), jnp.int32),
            pltpu.VMEM((block_rows, width), f32),
            pltpu.SMEM((block_rows, width), jnp.int32),
            pltpu.SMEM((block_rows, width), f32),
            pltpu.VMEM((peers, CAP, width), f32),
            pltpu.VMEM((peers, CAP, width), f32),
            exchange,
            exchange,
            exchange,
            exchange,
            gathers,
            gathers,
            gathers,
            pltpu.VMEM((2,) + right_side.shape, f32),
            pltpu.VMEM((2, 1, width), f32),
            pltpu.VMEM((2, peers, 1, width), f32),
            pltpu.VMEM((8, width), f32),
            pltpu.VMEM((n_cols - 1, 8, width), f32),
            *two_stages,
            *two_stages,
            *folded,
            *folded,
            pltpu.VMEM((1, width), f32),
            pltpu.VMEM((n_rows * n_cols - 1, 1, width), f32),
            pltpu.SemaphoreType.DMA((block_rows,)),
            pltpu.SemaphoreType.DMA((6,)),
            pltpu.SemaphoreType.DMA((3, peers)),
            pltpu.SemaphoreType.DMA((20,)),
            pltpu.SemaphoreType.DMA((20,)),
        ],
        compiler_params=pltpu.CompilerParams(
            collective_id=0, has_side_effects=True, vmem_limit_bytes=48 << 20
        ),
    )(
        in_hbm(hblocks),
        in_hbm(col_index),
        in_hbm(right_side),
        center,
        in_hbm(shifts.reshape(1, -1)),
        in_hbm(filter_weights.reshape(1, -1)),
    )
    filtered, gram, ritz = deliver(outputs)
    return filtered, gram.T, ritz.T


def solution(mesh):
    placed = (P("rows", None, None, None), P("rows", None), P("rows", "cols", None), P(), P(), P())
    n_rows, n_cols = mesh.shape["rows"], mesh.shape["cols"]

    def body(hblocks, col_index, right_side, *rest):
        block_rows, per_row, width = hblocks.shape[:3]
        vecs = right_side.shape[1]
        peers = n_rows - 1
        fits = (
            CAP * peers * block_rows <= block_rows * per_row
            and per_row + CAP * peers <= width
            and 2 * n_cols * vecs == width
            and width == 128
            and block_rows % 4 == 0
            and n_rows % 2 == 0
            and n_rows > 2
            and vecs % 16 == 0
        )
        if fits:
            return fused_shards(n_rows, n_cols, hblocks, col_index, right_side, *rest)
        return shards(hblocks, col_index, right_side, *rest)

    return jax.shard_map(
        body,
        mesh=mesh,
        in_specs=placed,
        out_specs=(P("rows", "cols", None), P(None, "cols"), P(None, "cols")),
        check_vma=False,
    )
```

```python
import functools

import jax
import jax.numpy as jnp
from jax import lax
from jax.experimental import pallas as pl
from jax.experimental.pallas import tpu as pltpu
from jax.sharding import PartitionSpec as P

CAP = 2


exact_mode = lax.Precision.HIGHEST


def column_dot(first_arr, second_arr):
    return jnp.sum(first_arr * second_arr, axis=(0, 2))


def ordered_lists(need_mask, slot_width):
    ranks = jnp.cumsum(need_mask, axis=1)
    positions = lax.broadcasted_iota(jnp.int32, need_mask.shape, 1)
    columns_out = []
    for slot in range(slot_width):
        hit = (need_mask > 0) & (ranks == slot + 1)
        columns_out.append(jnp.sum(jnp.where(hit, positions, 0), axis=1))
    lists = jnp.stack(columns_out, axis=1)
    live = jnp.sum(need_mask, axis=1, keepdims=True) > 0
    return jnp.where(live, lists, -1)


def filter_factors(alpha_one, beta_one, alpha_two, delta_shift, weights):
    zeta_one = 1.0 / (1.0 + delta_shift * alpha_one)
    zeta_two = (
        zeta_one
        * alpha_one
        / (alpha_two * beta_one * (1.0 - zeta_one) + alpha_one * (1.0 + delta_shift * alpha_two))
    )
    from_start = jnp.sum(
        weights * (alpha_one * zeta_one + alpha_two * beta_one * zeta_one * zeta_two), axis=0
    )
    from_residual = jnp.sum(weights * (alpha_two * zeta_two), axis=0)
    return from_start, from_residual


def shards(hblocks, col_index, right_side, center, shifts, filter_weights):
    block_rows = hblocks.shape[0]
    block_width = hblocks.shape[2]
    local_vecs = right_side.shape[1]
    pole_count = shifts.shape[0]
    peer_count = lax.axis_size("rows")
    slot_width = CAP
    device_index = lax.axis_index("rows")
    own_cols = col_index[:, :block_rows] - device_index * block_rows
    far_cols = col_index[:, block_rows:].reshape(-1)
    near_blocks = hblocks[:, :block_rows]
    far_blocks = hblocks[:, block_rows:]
    every_key = jnp.arange(peer_count * block_rows, dtype=jnp.int32)
    need_mask = (
        jnp.any(far_cols[:, None] == every_key[None, :], axis=0)
        .astype(jnp.int32)
        .reshape(peer_count, block_rows)
    )
    incoming_mask = lax.all_to_all(need_mask, "rows", split_axis=0, concat_axis=0, tiled=True)
    send_lists = ordered_lists(incoming_mask, slot_width)
    my_lists = ordered_lists(need_mask, slot_width)
    owners = lax.broadcasted_iota(jnp.int32, my_lists.shape, 0)
    slot_keys = jnp.where(my_lists >= 0, owners * block_rows + my_lists, -1).reshape(-1)
    slot_total = slot_keys.shape[0]
    matches = far_cols[:, None] == slot_keys[None, :]
    picker = matches.astype(jnp.float32)
    slot_numbers = lax.broadcasted_iota(jnp.int32, matches.shape, 1)
    slot_of_ref = jnp.sum(jnp.where(matches, slot_numbers, 0), axis=1)
    row_numbers = jnp.arange(block_rows, dtype=jnp.int32)[:, None]
    spread = (send_lists.reshape(-1)[None, :] == row_numbers).astype(jnp.float32)
    own_spread = (own_cols.reshape(-1)[None, :] == row_numbers).astype(jnp.float32)
    send_index = jnp.maximum(send_lists, 0)
    send_live = (send_lists >= 0)[:, :, None, None]

    def apply_h(vector):
        far_terms = jnp.einsum("ikab,iva->ikvb", far_blocks, vector, precision=exact_mode).reshape(
            far_cols.shape[0], -1
        )
        slot_sums = jnp.dot(picker.T, far_terms, precision=exact_mode).reshape(
            peer_count, slot_width, local_vecs, block_width
        )
        picked = vector[send_index]
        outgoing = jnp.where(send_live, picked, jnp.zeros_like(picked))
        both = lax.all_to_all(
            jnp.concatenate([outgoing, slot_sums], axis=1),
            "rows",
            split_axis=0,
            concat_axis=0,
            tiled=True,
        )
        arrived = both[:, :slot_width].reshape(slot_total, local_vecs, block_width)
        returned = both[:, slot_width:].reshape(slot_total, -1)
        near_vec = vector[own_cols]
        result = jnp.einsum("ikab,ikvb->iva", near_blocks, near_vec, precision=exact_mode)
        near_terms = jnp.einsum(
            "ikab,iva->ikvb", near_blocks, vector, precision=exact_mode
        ).reshape(block_rows * block_rows, -1)
        result = result + jnp.dot(own_spread, near_terms, precision=exact_mode).reshape(
            vector.shape
        )
        far_vec = arrived[slot_of_ref]
        far_vec = far_vec.reshape(block_rows, -1, local_vecs, block_width)
        result = result + jnp.einsum("ikab,ikvb->iva", far_blocks, far_vec, precision=exact_mode)
        return result + jnp.dot(spread, returned, precision=exact_mode).reshape(vector.shape)

    def wide(per_column):
        return per_column[None, :, None]

    center_value = center[0]
    base_shift = jnp.min(shifts)
    delta_shift = (shifts - base_shift)[:, None]
    start = right_side
    start_image = apply_h(start)
    half_one = start_image - center_value * start
    start_norm, half_norm = lax.psum(
        jnp.stack([column_dot(start, start), column_dot(half_one, half_one)]), "rows"
    )
    alpha_one = start_norm / (half_norm + base_shift * start_norm)
    op_image = apply_h(half_one) - center_value * half_one + base_shift * start
    residual = start - wide(alpha_one) * op_image
    residual_image = apply_h(residual)
    res_norm = lax.psum(column_dot(residual, residual), "rows")
    beta_one = res_norm / start_norm
    direction = residual + wide(beta_one) * start
    half_two = residual_image - center_value * residual + wide(beta_one) * half_one
    energy = lax.psum(
        column_dot(half_two, half_two) + base_shift * column_dot(direction, direction), "rows"
    )
    from_start, from_residual = filter_factors(
        alpha_one, beta_one, res_norm / energy, delta_shift, filter_weights[:, None]
    )
    filtered = wide(from_start) * start + wide(from_residual) * residual
    applied = wide(from_start) * start_image + wide(from_residual) * residual_image
    column_piece = lax.all_gather(filtered, "cols", axis=1, tiled=True)
    correlation = jnp.einsum("iae,ibe->ab", column_piece, filtered, precision=exact_mode)
    projected = jnp.einsum("iae,ibe->ab", column_piece, applied, precision=exact_mode)
    partial_gram = jnp.stack([correlation, projected])
    summed = lax.psum(partial_gram, "rows")
    row_total = peer_count * block_rows * block_width
    return (filtered, summed[0] / row_total, summed[1] / row_total)


def split(value):
    high = value.astype(jnp.bfloat16)
    low = (value - high.astype(jnp.float32)).astype(jnp.bfloat16)
    return high, low


def lane_sum(value):
    return jnp.sum(value, axis=1, keepdims=True)


def row_sum(value):
    return jnp.sum(value, axis=0, keepdims=True)


HALF_GAP = 32
SPOT_GAP = 16


def filter_kernel(n_rows, n_cols, refs, accumulators):
    (
        blocks_hbm,
        cols_hbm,
        vec_hbm,
        center_ref,
        shifts_hbm,
        weights_hbm,
        out_ref,
        gram_ref,
        ritz_ref,
        *scratch,
    ) = refs
    block_rows, vecs, width = out_ref.shape
    per_row = blocks_hbm.shape[1]
    row_blocks, scratch = scratch[:block_rows], scratch[block_rows:]
    (
        cols_vmem,
        vec_ref,
        shifts_vmem,
        weights_vmem,
        high,
        low,
        running,
        index_vmem,
        mask_vmem,
        index_smem,
        mask_smem,
        lists_send,
        lists,
        vec_send,
        vec_recv,
        prod_send,
        prod_recv,
        col_start,
        col_image,
        col_second,
        image_send,
        sums_send,
        sums_recv,
        known_send,
        known_recv,
        early_send,
        early_recv,
        early_half,
        early_other,
        middle_send,
        middle_recv,
        middle_half,
        middle_other,
        square_send,
        square_recv,
        last_send,
        last_recv,
        energy_send,
        energy_recv,
        load_sems,
        small_sems,
        vec_sems,
        send_sems,
        recv_sems,
    ) = scratch
    totals, terms, grams = accumulators
    far = per_row - block_rows
    mine = block_rows * width
    peers = n_rows - 1
    slots = CAP * peers
    near_peers = n_rows // 2
    count = n_cols * vecs
    me = lax.axis_index("rows")
    me_col = lax.axis_index("cols")
    drains = []
    used = [0]

    smalls = [
        pltpu.make_async_copy(src, dst, small_sems.at[i])
        for i, (src, dst) in enumerate(
            [
                (cols_hbm, cols_vmem),
                (vec_hbm, vec_ref),
                (shifts_hbm, shifts_vmem),
                (weights_hbm, weights_vmem),
            ]
        )
    ]
    smalls[0].start()
    loads = [
        pltpu.make_async_copy(blocks_hbm.at[row], row_blocks[row], load_sems.at[row])
        for row in range(block_rows)
    ]
    loads[0].start()
    barrier = pltpu.get_barrier_semaphore()
    for step in range(1, n_rows):
        pl.semaphore_signal(barrier, inc=1, device_id={"rows": lax.rem(me + step, n_rows)})
    for step in range(1, n_cols):
        pl.semaphore_signal(barrier, inc=1, device_id={"cols": lax.rem(me_col + step, n_cols)})

    def begin(src, dst, send, recv, where):
        pltpu.make_async_remote_copy(
            src_ref=src,
            dst_ref=dst,
            send_sem=send,
            recv_sem=recv,
            device_id=where,
            device_id_type=pl.DeviceIdType.MESH,
        ).start()

    def row_at(step):
        return {"rows": lax.rem(me + step, n_rows)}

    def partner(step):
        place, bit = me, 1
        while bit < n_rows:
            if step & bit:
                place = place + bit - 2 * bit * lax.rem(lax.div(me, bit), 2)
            bit *= 2
        return place

    def mate(step):
        return {"rows": partner(step)}

    def col_at(step):
        return {"cols": lax.rem(me_col + step, n_cols)}

    def bytes_of(ref, sem):
        return pltpu.make_async_copy(ref, ref, sem)

    def group(size):
        number = used[0]
        used[0] += 1
        send, recv = send_sems.at[number], recv_sems.at[number]
        drains.append(bytes_of(size, send))
        return send, recv, bytes_of(size, recv)

    def to_all(source, recv_ref):
        send, recv, landed = group(recv_ref)
        for step in range(peers, 0, -1):
            begin(source(step), recv_ref.at[step - 1], send, recv, mate(step))
        return landed

    def to_cols(source, recv_ref):
        send, recv, landed = group(recv_ref)
        for step in range(1, n_cols):
            begin(source, recv_ref.at[n_cols - 1 - step], send, recv, col_at(step))
        return landed

    smalls[0].wait()
    for copy in loads[1:] + smalls[1:]:
        copy.start()
    columns = cols_vmem[...]
    place = lax.broadcasted_iota(jnp.int32, columns.shape, 1)
    is_far = place >= block_rows
    inside = []
    for step in range(1, n_rows):
        inner = columns - partner(step) * block_rows
        hit = is_far & (inner >= 0) & (inner < block_rows)
        value = inner.astype(jnp.float32)
        first = jnp.min(jnp.where(hit, value, float(block_rows)), axis=0, keepdims=True)
        first = jnp.min(first, axis=1, keepdims=True)
        last = jnp.max(jnp.where(hit, value, -1.0), axis=0, keepdims=True)
        last = jnp.max(last, axis=1, keepdims=True)
        lists_send[step - 1, 0:1, :] = jnp.broadcast_to(first, (1, width))
        lists_send[step - 1, 1:2, :] = jnp.broadcast_to(last, (1, width))
        inside.append((hit, inner, last))
    pl.semaphore_wait(barrier, peers + n_cols - 1)
    lists_landed = to_all(lambda step: lists_send.at[step - 1], lists)

    def place_blocks():
        lane = lax.broadcasted_iota(jnp.int32, (block_rows, width), 1)
        own = columns - me * block_rows
        slot = jnp.full(columns.shape, -1, jnp.int32)
        for number, (hit, inner, last) in enumerate(inside):
            upper = (inner == last.astype(jnp.int32)).astype(jnp.int32)
            slot = jnp.where(hit, CAP * number + upper, slot)
        key = slot * per_row + place
        rank = jnp.zeros(columns.shape, jnp.int32)
        follows = jnp.zeros(columns.shape, jnp.int32)
        for k in range(block_rows, per_row):
            rank = rank + (key[:, k : k + 1] < key).astype(jnp.int32)
            same = (slot[:, k : k + 1] == slot) & (place > k)
            follows = follows | same.astype(jnp.int32)
        order = jnp.zeros(lane.shape, jnp.int32)
        keep = jnp.zeros(lane.shape, jnp.int32)
        ends = jnp.full(lane.shape, -1, jnp.int32)
        live = jnp.zeros(lane.shape, jnp.int32)
        for k in range(block_rows):
            order = order + jnp.where(own[:, k : k + 1] == lane, k, 0)
        for k in range(block_rows, per_row):
            here = rank[:, k : k + 1] == lane - block_rows
            order = order + jnp.where(here, k, 0)
            keep = keep + jnp.where(here, follows[:, k : k + 1], 0)
            ends = ends + (slot[:, k : k + 1] <= lane - per_row).astype(jnp.int32)
            live = live | (slot[:, k : k + 1] == lane - per_row).astype(jnp.int32)
        tail = lane >= per_row
        ends = jnp.minimum(jnp.maximum(ends, 0), far - 1)
        index_vmem[...] = jnp.where(tail, ends, jnp.minimum(order, per_row - 1))
        mask_vmem[...] = jnp.where(tail, live, keep).astype(jnp.float32)
        moves = [
            pltpu.make_async_copy(index_vmem, index_smem, small_sems.at[4]),
            pltpu.make_async_copy(mask_vmem, mask_smem, small_sems.at[5]),
        ]
        for move in moves:
            move.start()
        return moves

    moves = place_blocks()
    for move in moves:
        move.wait()

    chunk = running.shape[1]
    half_rows = block_rows // 2
    for row in range(block_rows):
        loads[row].wait()
        source = row_blocks[row]
        base_line = row * width + (HALF_GAP if row >= half_rows else 0)

        @pl.loop(0, width // chunk)
        def _(part):
            lines = pl.ds(pl.multiple_of(part * chunk, chunk), chunk)
            target = pl.ds(pl.multiple_of(base_line + part * chunk, 16), chunk)

            def put(spot, value):
                top, bottom = split(value)
                high[spot, target, :] = top
                low[spot, target, :] = bottom

            total = jnp.zeros((chunk, width), jnp.float32)
            for j in range(far):
                block = source[index_smem[row, block_rows + j], lines, :]
                total = total * mask_smem[row, block_rows + j] + block
                running[j] = total
            for spot in range(block_rows):
                put(spot, source[index_smem[row, spot], lines, :])
            for s in range(slots):
                value = running[index_smem[row, per_row + s]] * mask_smem[row, per_row + s]
                put(block_rows + s, value)

    tile = 2 * width
    tiles = block_rows // 2
    staged = [0, 0]

    def feed(unit, weights, transposed, uses):
        register = staged[unit]
        staged[unit] = 1 - register
        pltpu.matmul_push_rhs(weights, register, unit, transpose=transposed)
        for number, (acc, rows) in enumerate(uses):
            pltpu.matmul_acc_lhs(acc, rows, register if number == 0 else None)

    def block(ref, spot, lines):
        begin_at = lines * tile + (HALF_GAP if lines >= tiles // 2 else 0)
        first = slice(begin_at, begin_at + tile)
        return jnp.concatenate([ref[spot, first, :], ref[spot + 1, first, :]], axis=1)

    def multiply(unit, acc, parts, spot, lines, at, transposed):
        top, bottom = [part[:, at * tile : (at + 1) * tile] for part in parts]
        feed(unit, block(high, spot, lines), transposed, [(acc, top), (acc, bottom)])
        feed(unit, block(low, spot, lines), transposed, [(acc, top)])

    half_tiles = tiles // 2

    def sum_of(n):
        return totals[n // half_tiles][n % half_tiles]

    woven = [n + u * half_tiles for n in range(half_tiles) for u in range(2)]

    def flat(ref):
        return jnp.concatenate([ref[i] for i in range(block_rows)], axis=1)

    def piece(value, row):
        return value[:, row * width : (row + 1) * width]

    def named(step, slot, row):
        return jnp.broadcast_to(lists[step - 1, slot : slot + 1, :], (vecs, width)) == float(row)

    lane_of = lax.broadcasted_iota(jnp.int32, (vecs, width), 1)
    row_of = lax.broadcasted_iota(jnp.int32, (vecs, width), 0)

    def as_row(value, first):
        return row_sum(jnp.where(lane_of == row_of + first, value, 0.0))

    def as_column(row_value, first):
        return lane_sum(jnp.where(lane_of == row_of + first, row_value, 0.0))

    def send_sums(turn, values):
        packed = as_row(values[0], 0)
        for q, value in enumerate(values[1:]):
            packed = packed + as_row(value, (q + 1) * vecs)
        sums_send[turn] = packed
        return to_all(lambda step: sums_send.at[turn], sums_recv.at[turn])

    def total_sums(turn, landed, quantities):
        landed.wait()
        total = sums_send[turn]
        for step in range(1, n_rows):
            total = total + sums_recv[turn, step - 1]
        return [as_column(total, q * vecs) for q in range(quantities)]

    def send_vectors(turn, vector):
        number = used[0]
        used[0] += 1
        send = send_sems.at[number]
        drains.append(bytes_of(vec_send.at[turn], send))
        for step in range(peers, 0, -1):
            for slot in range(CAP):
                picked = jnp.zeros((vecs, width), jnp.float32)
                for row in range(block_rows):
                    picked = jnp.where(named(step, slot, row), piece(vector, row), picked)
                vec_send[turn, step - 1, :, slot * width : (slot + 1) * width] = picked
            begin(
                vec_send.at[turn, step - 1],
                vec_recv.at[turn, step - 1],
                send,
                vec_sems.at[turn, step - 1],
                mate(step),
            )

    def send_products(turn, parts):
        send, recv, landed = group(prod_recv.at[turn])

        def launch(ready):
            for step, accs in ready:
                value = functools.reduce(jnp.add, [pltpu.matmul_pop(acc) for acc in accs])
                prod_send[turn, step - 1] = value
                begin(
                    prod_send.at[turn, step - 1],
                    prod_recv.at[turn, step - 1],
                    send,
                    recv,
                    mate(step),
                )

        ready = []
        for first in range(peers, 0, -2):
            which = (first // 2) % 2
            even, odd = terms[0][which], terms[1][which]
            spot = block_rows + CAP * (first - 1)
            if first + 1 < n_rows:
                for lines in range(tiles):
                    multiply(0, even, parts, spot, lines, lines, False)
                    multiply(1, odd, parts, spot + CAP, lines, lines, False)
                done = [(first, [even]), (first + 1, [odd])]
            else:
                for lines in range(half_tiles):
                    later = lines + half_tiles
                    multiply(0, even, parts, spot, lines, lines, False)
                    multiply(1, odd, parts, spot, later, later, False)
                done = [(first, [even, odd])]
            launch(ready)
            ready = done
        launch(ready)
        return landed

    def local(parts):
        for at in range(tiles):
            for n in woven:
                line = (at + n // half_tiles * half_tiles) % tiles
                multiply(n // half_tiles, sum_of(n), parts, 2 * n, line, line, False)
        for at in range(tiles):
            for n in woven:
                multiply(n // half_tiles, sum_of(n), parts, 2 * at, n, at, True)

    def take_vectors(turn):
        for step in range(1, n_rows):
            bytes_of(vec_recv.at[turn, step - 1], vec_sems.at[turn, step - 1]).wait()
            parts = split(vec_recv[turn, step - 1])
            spot = block_rows + CAP * (step - 1)
            for n in woven:
                multiply(n // half_tiles, sum_of(n), parts, spot, n, 0, True)
        return [pltpu.matmul_pop(sum_of(n)) for n in range(tiles)]

    def take_products(turn, halves, landed):
        result = jnp.concatenate(halves, axis=1)
        pieces = [piece(result, row) for row in range(block_rows)]
        landed.wait()
        for step in range(1, n_rows):
            for slot in range(CAP):
                back = prod_recv[turn, step - 1, :, slot * width : (slot + 1) * width]
                for row in range(block_rows):
                    pieces[row] = pieces[row] + jnp.where(named(step, slot, row), back, 0.0)
        return jnp.concatenate(pieces, axis=1)

    def gathered(own, recv):
        start_at = me_col
        pieces = []
        for c in range(n_cols):
            total = jnp.where(start_at == c, own, 0.0)
            for step in range(1, n_cols):
                other = flat(recv.at[step - 1])
                total = jnp.where(lax.rem(start_at + step, n_cols) == c, other, total)
            pieces.append(total)
        return split(jnp.concatenate(pieces, axis=0))

    def share_columns(number, value, recv_ref):
        for row in range(block_rows):
            image_send[number, row] = piece(value, row)
        return to_cols(image_send.at[number], recv_ref)

    def against(pieces, every):
        top, bottom = split(jnp.concatenate(pieces, axis=0))
        rows = jnp.concatenate([top, bottom], axis=0)
        weights = [part for parts_of in every for part in parts_of]
        weights += [jnp.zeros_like(weights[0])] * (tile // count - len(weights))
        accs = [grams[u][len(pieces) - 1] for u in range(2)]
        for at in range(mine // tile):
            lines = slice(at * tile, (at + 1) * tile)
            tall = jnp.concatenate([weight[:, lines] for weight in weights], axis=0)
            feed(at % 2, tall, True, [(accs[at % 2], rows[:, lines])])
        both = pltpu.matmul_pop(accs[0]) + pltpu.matmul_pop(accs[1])
        half = top.shape[0]
        results = []
        for number in range(len(every)):
            at = 2 * number * count
            wide_part = both[:half, at : at + count] + both[:half, at + count : at + 2 * count]
            results.append(wide_part + both[half:, at : at + count])
        return results

    def to_half(source, recv_ref):
        send, recv, landed = group(recv_ref)
        for step in range(1, near_peers):
            begin(source, recv_ref.at[step - 1], send, recv, mate(step))
        return landed

    def to_mirror(landed, own_ref, recv_ref, half_ref, other_ref):
        landed.wait()
        half_ref[...] = summed(own_ref, recv_ref)
        send, recv, crossed = group(other_ref)
        begin(half_ref, other_ref, send, recv, row_at(near_peers))
        return crossed

    def summed(own_ref, recv):
        total = own_ref[...]
        for number in range(recv.shape[0]):
            total = total + recv[number]
        return total

    for copy in smalls[1:]:
        copy.wait()
    center = center_ref[0]
    base = jnp.min(shifts_vmem[...], axis=1, keepdims=True)
    start = flat(vec_ref)

    lists_landed.wait()
    send_vectors(0, start)
    start_landed = to_cols(vec_ref, col_start)
    parts = split(start)
    products = send_products(0, parts)
    local(parts)
    halves = take_vectors(0)
    image = take_products(0, halves, products)

    half = image - center * start
    send_vectors(1, half)
    sums_landed = send_sums(0, [lane_sum(start * start), lane_sum(half * half)])
    image_landed = share_columns(0, image, col_image)
    parts = split(half)
    products = send_products(1, parts)
    local(parts)
    start_landed.wait()
    every_start = gathered(start, col_start)
    early = against([start, image], [every_start])[0]
    early_send[...] = jnp.concatenate([early[:vecs], early[vecs:]], axis=1)
    early_landed = to_half(early_send, early_recv)
    halves = take_vectors(1)
    start_norm, half_norm = total_sums(0, sums_landed, 2)
    alpha = start_norm / (half_norm + base * start_norm)
    applied = take_products(1, halves, products)

    second = applied - center * half
    residual = start - alpha * (second + base * start)
    send_vectors(2, residual)
    norm_landed = send_sums(1, [lane_sum(residual * residual)])
    second_landed = share_columns(1, second, col_second)
    parts = split(residual)
    products = send_products(2, parts)
    early_crossed = to_mirror(early_landed, early_send, early_recv, early_half, early_other)
    image_landed.wait()
    every_image = gathered(image, col_image)
    middle_send[...] = jnp.concatenate(against([second], [every_start, every_image]), axis=1)
    middle_landed = to_half(middle_send, middle_recv)
    local(parts)
    halves = take_vectors(2)

    half_vecs = vecs // 2

    def folded(value):
        return jnp.concatenate([value[:half_vecs], value[half_vecs:]], axis=1)

    def unfolded(value):
        return jnp.concatenate([value[:, :count], value[:, count:]], axis=0)

    (res_norm,) = total_sums(1, norm_landed, 1)
    beta = res_norm / start_norm
    direction = residual + beta * start
    rest = beta * half - center * residual
    own_base = lane_sum(base * (direction * direction))
    spot = me_col * vecs
    known = [as_row(value, spot) for value in (alpha, beta, res_norm)]
    known_send[...] = jnp.concatenate(
        known + [jnp.zeros((8 - len(known), width), jnp.float32)], axis=0
    )
    known_landed = to_cols(known_send, known_recv)
    final_image = take_products(2, halves, products)

    half_two = final_image + rest
    energy_send[...] = as_row(own_base + lane_sum(half_two * half_two), spot)
    send, recv, energy_landed = group(energy_recv)
    for row_step in range(n_rows - 1, -1, -1):
        for col_step in range(n_cols):
            if row_step == 0 and col_step == 0:
                continue
            opposite = ((n_rows - row_step) % n_rows) * n_cols + (n_cols - col_step) % n_cols - 1
            begin(
                energy_send,
                energy_recv.at[opposite],
                send,
                recv,
                {**row_at(row_step), **col_at(col_step)},
            )
    second_landed.wait()
    every_second = gathered(second, col_second)
    last_send[...] = folded(against([final_image], [every_second])[0])
    last_landed = to_all(lambda step: last_send, last_recv)
    square_send[...] = folded(against([second], [every_second])[0])
    square_landed = to_all(lambda step: square_send, square_recv)
    middle_crossed = to_mirror(middle_landed, middle_send, middle_recv, middle_half, middle_other)

    settled, drains[:] = drains[:], []
    for drain in settled[:-4]:
        drain.wait()
    drains.extend(settled[-4:])
    early_crossed.wait()
    early_total = early_half[...] + early_other[...]
    known_landed.wait()
    shared = summed(known_send, known_recv)
    live = lax.broadcasted_iota(jnp.int32, (1, width), 1) < count
    alpha_one, beta_one, norm_two = [
        jnp.where(live, shared[q : q + 1], 1.0) for q in range(3)
    ]
    poles = []
    for m in range(shifts_vmem.shape[1]):
        delta = shifts_vmem[:, m : m + 1] - base
        weight = weights_vmem[:, m : m + 1]
        zeta_one = 1.0 / (1.0 + delta * alpha_one)
        slope = beta_one * (1.0 - zeta_one) + alpha_one * delta
        poles.append((weight, zeta_one, slope))
    middle_crossed.wait()
    middle_total = middle_half[...] + middle_other[...]
    square_landed.wait()
    squares = unfolded(summed(square_send, square_recv))
    crossed, paired = middle_total[:, :count], middle_total[:, count:]
    plain, rayleigh = early_total[:, :count], early_total[:, count:]

    energy_landed.wait()
    alpha_two = norm_two / jnp.where(live, summed(energy_send, energy_recv), 1.0)
    from_start = jnp.zeros((1, width), jnp.float32)
    from_residual = from_start
    for weight, zeta_one, slope in poles:
        zeta_two = zeta_one * alpha_one / (alpha_one + alpha_two * slope)
        from_start = from_start + weight * (
            alpha_one * zeta_one + alpha_two * beta_one * zeta_one * zeta_two
        )
        from_residual = from_residual + weight * (alpha_two * zeta_two)
    on_start = from_start + from_residual * (1.0 - alpha_one * base)
    on_image = -from_residual * alpha_one

    first_b = as_column(from_start, spot)
    residual_b = as_column(from_residual, spot)
    start_b = first_b + residual_b * (1.0 - alpha * base)
    image_b = -residual_b * alpha
    filtered = first_b * start + residual_b * residual
    for row in range(block_rows):
        out_ref[row] = piece(filtered, row)
    start_a, image_a = on_start[:, :count], on_image[:, :count]
    scale = 1.0 / (n_rows * mine)
    gram_ref[...] = scale * (
        start_b * start_a * plain
        + (start_b * image_a + image_b * start_a) * crossed
        + image_b * image_a * squares
    )
    last_landed.wait()
    closing = unfolded(summed(last_send, last_recv))
    ritz_ref[...] = scale * (
        start_b * start_a * rayleigh
        + (first_b * image_a + image_b * start_a) * paired
        + residual_b * image_a * closing
    )
    for drain in drains:
        drain.wait()


def scoped_kernel(n_rows, n_cols, *refs):
    block_rows, vecs, width = refs[6].shape

    def accumulators(rows):
        return [
            [pltpu.ACC(unit)((count, 2 * width), jnp.float32) for count in rows]
            for unit in range(2)
        ]

    pl.run_scoped(
        lambda *accs: filter_kernel(n_rows, n_cols, refs, accs),
        accumulators([vecs] * (block_rows // 4)),
        accumulators([vecs] * 2),
        accumulators([2 * vecs * pieces for pieces in (1, 2)]),
    )


def deliver_kernel(*refs):
    sems = refs[-1]
    half = (len(refs) - 1) // 2
    copies = [
        pltpu.make_async_copy(refs[i], refs[half + i], sems.at[i]) for i in range(half)
    ]
    for copy in copies:
        copy.start()
    for copy in copies:
        copy.wait()


def deliver(arrays):
    return pl.pallas_call(
        deliver_kernel,
        out_shape=[jax.ShapeDtypeStruct(a.shape, a.dtype) for a in arrays],
        in_specs=[pl.BlockSpec(memory_space=pltpu.VMEM)] * len(arrays),
        out_specs=[pl.BlockSpec(memory_space=pltpu.HBM)] * len(arrays),
        scratch_shapes=[pltpu.SemaphoreType.DMA((len(arrays),))],
        compiler_params=pltpu.CompilerParams(vmem_limit_bytes=1 << 20),
    )(*arrays)


def in_hbm(value):
    return pltpu.with_memory_space_constraint(value, pltpu.HBM)


def fused_shards(
    n_rows, n_cols, hblocks, col_index, right_side, center, shifts, filter_weights
):
    block_rows, per_row, width, _ = hblocks.shape
    vecs = right_side.shape[1]
    peers = n_rows - 1
    near_peers = n_rows // 2
    slots = CAP * peers
    far = per_row - block_rows
    mine = block_rows * width
    columns = n_cols * vecs
    pair = CAP * width
    chunk = 32
    vmem = pl.BlockSpec(memory_space=pltpu.VMEM)
    hbm = pl.BlockSpec(memory_space=pltpu.HBM)
    f32 = jnp.float32
    exchange = pltpu.VMEM((3, peers, vecs, pair), f32)
    packed = pltpu.VMEM((block_rows + slots, mine + HALF_GAP + SPOT_GAP, width), jnp.bfloat16)
    gathers = pltpu.VMEM((n_cols - 1,) + right_side.shape, f32)
    product = pltpu.VMEM((vecs, 2 * columns), f32)
    two_stages = [
        product,
        pltpu.VMEM((near_peers - 1, vecs, 2 * columns), f32),
        product,
        product,
    ]
    folded = [
        pltpu.VMEM((vecs // 2, 2 * columns), f32),
        pltpu.VMEM((peers, vecs // 2, 2 * columns), f32),
    ]
    outputs = pl.pallas_call(
        functools.partial(scoped_kernel, n_rows, n_cols),
        out_shape=[
            jax.ShapeDtypeStruct(right_side.shape, f32),
            jax.ShapeDtypeStruct((vecs, columns), f32),
            jax.ShapeDtypeStruct((vecs, columns), f32),
        ],
        in_specs=[hbm, hbm, hbm, pl.BlockSpec(memory_space=pltpu.SMEM), hbm, hbm],
        out_specs=[vmem, vmem, vmem],
        scratch_shapes=[pltpu.VMEM((per_row, width, width), f32)] * block_rows
        + [
            pltpu.VMEM(col_index.shape, jnp.int32),
            pltpu.VMEM(right_side.shape, f32),
            pltpu.VMEM((1, shifts.shape[0]), f32),
            pltpu.VMEM((1, shifts.shape[0]), f32),
            packed,
            packed,
            pltpu.VMEM((far, chunk, width), f32),
            pltpu.VMEM((block_rows, width), jnp.int32),
            pltpu.VMEM((block_rows, width), f32),
            pltpu.SMEM((block_rows, width), jnp.int32),
            pltpu.SMEM((block_rows, width), f32),
            pltpu.VMEM((peers, CAP, width), f32),
            pltpu.VMEM((peers, CAP, width), f32),
            exchange,
            exchange,
            exchange,
            exchange,
            gathers,
            gathers,
            gathers,
            pltpu.VMEM((2,) + right_side.shape, f32),
            pltpu.VMEM((2, 1, width), f32),
            pltpu.VMEM((2, peers, 1, width), f32),
            pltpu.VMEM((8, width), f32),
            pltpu.VMEM((n_cols - 1, 8, width), f32),
            *two_stages,
            *two_stages,
            *folded,
            *folded,
            pltpu.VMEM((1, width), f32),
            pltpu.VMEM((n_rows * n_cols - 1, 1, width), f32),
            pltpu.SemaphoreType.DMA((block_rows,)),
            pltpu.SemaphoreType.DMA((6,)),
            pltpu.SemaphoreType.DMA((3, peers)),
            pltpu.SemaphoreType.DMA((20,)),
            pltpu.SemaphoreType.DMA((20,)),
        ],
        compiler_params=pltpu.CompilerParams(
            collective_id=0, has_side_effects=True, vmem_limit_bytes=48 << 20
        ),
    )(
        in_hbm(hblocks),
        in_hbm(col_index),
        in_hbm(right_side),
        center,
        in_hbm(shifts.reshape(1, -1)),
        in_hbm(filter_weights.reshape(1, -1)),
    )
    filtered, gram, ritz = deliver(outputs)
    return filtered, gram.T, ritz.T


def solution(mesh):
    placed = (P("rows", None, None, None), P("rows", None), P("rows", "cols", None), P(), P(), P())
    n_rows, n_cols = mesh.shape["rows"], mesh.shape["cols"]

    def body(hblocks, col_index, right_side, *rest):
        block_rows, per_row, width = hblocks.shape[:3]
        vecs = right_side.shape[1]
        peers = n_rows - 1
        fits = (
            CAP * peers * block_rows <= block_rows * per_row
            and per_row + CAP * peers <= width
            and 2 * n_cols * vecs == width
            and width == 128
            and block_rows % 4 == 0
            and n_rows > 2
            and n_rows & (n_rows - 1) == 0
            and vecs % 16 == 0
        )
        if fits:
            return fused_shards(n_rows, n_cols, hblocks, col_index, right_side, *rest)
        return shards(hblocks, col_index, right_side, *rest)

    return jax.shard_map(
        body,
        mesh=mesh,
        in_specs=placed,
        out_specs=(P("rows", "cols", None), P(None, "cols"), P(None, "cols")),
        check_vma=False,
    )
```
